32 devices in a mesh: gx: 4 (over y, x), gy: 8 (over z, core).
Axes of the slice: x: 2, y: 2, z: 4, core: 2. Of those that a mesh axis runs over, the one named last changes fastest.
Arguments:
- node_shift: float32 [2, 256, 4096], P(None, 'gx', 'gy'), may hold values from -1.5 to 1.5
- node_speed: float32 [2, 256, 4096], P(None, 'gx', 'gy'), may hold values from -4 to 4
- damage_initial: int32 [2, 256, 4096], P(None, 'gx', 'gy'), may hold values from 0 to 7
- cohesive_markers: int32 [32, 8], P('gx', 'gy'), may hold values from 0 to 1, as said below
- cell_warmth: float32 [128, 2048], P(('gx', 'gy')), may hold values from 0 to 1
- heat_storage: float32 [128, 2048], P(('gx', 'gy')), may hold values from 0.5 to 2
- surface_transfer: float32 [128, 2048], P(('gx', 'gy')), may hold values from 0.1 to 1
- quench_liquid_heat: float32 [128, 2048], P(('gx', 'gy')), may hold values from 0 to 0.3
Outputs:
- displace_new: float32 [2, 256, 4096], P(None, 'gx', 'gy')
- velocity_new: float32 [2, 256, 4096], P(None, 'gx', 'gy')
- damage: bfloat16 [2, 256, 4096], P(None, 'gx', 'gy')
- warmth_after_solve: float32 [128, 2048], P(('gx', 'gy'))
The draws below stay inside these ranges and needn't reach their ends.
Inputs may be any that keep to these rules, and one draw needn't show every extreme that they name: `cohesive_markers`: within each column, every block of 8 consecutive tile rows starting at a multiple of 8 holds between 1 and 4 ones, and in every draw some block holds exactly 4.
All inputs are finite; a program needn't handle non-finite values.
Results may differ from the reference program's by a relative error of at most 0.001.
Values sent between devices are 32-bit elements; how exact they have to be, the bound alone decides.
A program may use at most 64 MiB of HBM per device.

```python
import math
import jax
import jax.numpy as jnp
from jax import lax

FX = 64
FY = 512
SR = 8
SEG = 128
SUBSTEPS = 8
ITERS = 4
NXF = 256
NYF = 4096
CELL_HEIGHT_NUM = 128
CELL_WIDTH_NUM = 2048
STRIPS = 8
MOST = 4
N_GX = 4
N_GY = 8


def marker_grid(key):
    block_total = NXF // FX * N_GY
    key_count, key_force, key_order = jax.random.split(jax.random.fold_in(key, 11), 3)
    counts = jax.random.randint(key_count, (block_total,), 1, MOST + 1)
    forced = jax.random.randint(key_force, (), 0, block_total)
    counts = jnp.where(jnp.arange(block_total) == forced, MOST, counts)
    orders = jax.vmap(lambda subkey: jax.random.permutation(subkey, STRIPS))(jax.random.split(key_order, block_total))
    marking = (orders < counts[:, None]).astype(jnp.int32)
    grid_marks = marking.reshape(NXF // FX, N_GY, STRIPS)
    return jnp.transpose(grid_marks, (0, 2, 1)).reshape(NXF // SR, N_GY)


def draw_cohesive_markers(key, part):
    return marker_grid(key)


def draw_damage_initial(key, part):
    key_level, key_keep = jax.random.split(jax.random.fold_in(key, 23))
    levels = jax.random.randint(key_level, (2, NXF, NYF), 0, 8)
    keeping = jax.random.randint(key_keep, (2, NXF, NYF), 0, 4)
    return jnp.where(keeping == 0, levels, 0).astype(jnp.int32)


def draw_node_speed(key, part):
    key_phase, key_rough = jax.random.split(jax.random.fold_in(key, 31))
    phases = jax.random.uniform(key_phase, (4,), jnp.float32)
    rows = jnp.arange(NXF, dtype=jnp.float32)[:, None]
    cols = jnp.arange(NYF, dtype=jnp.float32)[None, :]
    two_pi = 2.0 * math.pi
    amplitude = 1.6
    rough = jnp.clip(0.25 * jax.random.normal(key_rough, (2, NXF, NYF), jnp.float32), -1.0, 1.0)
    along_rows = amplitude * jnp.sin(two_pi * (rows / 32.0 + phases[0])) * (1.0 + 0.5 * jnp.sin(two_pi * (cols / 64.0 + phases[1])))
    along_cols = amplitude * jnp.sin(two_pi * (cols / 32.0 + phases[2])) * (1.0 + 0.5 * jnp.sin(two_pi * (rows / 64.0 + phases[3])))
    return (jnp.stack([along_rows, along_cols]) + rough).astype(jnp.float32)


def draw_heat_storage(key, part):
    marks = marker_grid(key)
    row_tile = 2 * jnp.arange(CELL_HEIGHT_NUM, dtype=jnp.int32) // SR
    col_tile = 2 * jnp.arange(CELL_WIDTH_NUM, dtype=jnp.int32) // FY
    coarse_marks = marks[row_tile][:, col_tile]
    fraction = jax.random.uniform(jax.random.fold_in(key, 41), (CELL_HEIGHT_NUM, CELL_WIDTH_NUM), jnp.float32)
    lower = jnp.where(coarse_marks == 1, math.log(0.5), math.log(1.25))
    upper = jnp.where(coarse_marks == 1, math.log(1.0), math.log(2.0))
    return jnp.exp(lower + (upper - lower) * fraction).astype(jnp.float32)


def shard_levels(stream_key, shape, cuts, smallest, largest):
    gain = 1.0
    for dim, blocks in cuts:
        steps = jax.random.uniform(jax.random.fold_in(jax.random.fold_in(stream_key, 6), dim), (blocks,), jnp.float32, smallest / len(cuts), largest / len(cuts))
        gain = gain * jnp.repeat(jnp.exp(steps), shape[dim] // blocks).reshape((-1,) + (1,) * (len(shape) - 1 - dim))
    return gain


def bell_draw(own_key, extent, width, most, cuts=(), held_as=jnp.bfloat16):
    result = width * jax.random.normal(own_key, extent, jnp.float32)
    if cuts:
        result = result * shard_levels(own_key, extent, cuts, -0.22, 0.18)
    return jnp.clip(result, -most, most).astype(held_as)


def setup_inputs(seed: int = 0) -> dict:
    key_of = jax.random.split(jax.random.key(seed), 9)
    node_shift = bell_draw(key_of[0], (2, NXF, NYF), 0.1, 1.5, ((1, 4), (2, 8)), jnp.float32)
    node_speed = draw_node_speed(jax.random.fold_in(key_of[8], 71), 0)
    damage_initial = draw_damage_initial(jax.random.fold_in(key_of[8], 71), 0)
    cohesive_markers = draw_cohesive_markers(jax.random.fold_in(key_of[8], 71), 0)
    cell_warmth = jnp.clip(1.0 * jax.random.uniform(key_of[4], (CELL_HEIGHT_NUM, CELL_WIDTH_NUM), jnp.float32) ** shard_levels(key_of[4], (CELL_HEIGHT_NUM, CELL_WIDTH_NUM), ((0, 32),), -0.2, 0.2), 0.0, 1.0)
    heat_storage = draw_heat_storage(jax.random.fold_in(key_of[8], 71), 0)
    surface_transfer = jnp.clip(0.1 + 0.9 * jax.random.uniform(key_of[6], (CELL_HEIGHT_NUM, CELL_WIDTH_NUM), jnp.float32) ** shard_levels(key_of[6], (CELL_HEIGHT_NUM, CELL_WIDTH_NUM), ((0, 32),), -0.2, 0.2), 0.1, 1.0)
    quench_liquid_heat = jnp.clip(0.3 * jax.random.uniform(key_of[7], (CELL_HEIGHT_NUM, CELL_WIDTH_NUM), jnp.float32) ** shard_levels(key_of[7], (CELL_HEIGHT_NUM, CELL_WIDTH_NUM), ((0, 32),), -0.2, 0.2), 0.0, 0.3)
    return dict(node_shift=node_shift, node_speed=node_speed, damage_initial=damage_initial, cohesive_markers=cohesive_markers, cell_warmth=cell_warmth, heat_storage=heat_storage, surface_transfer=surface_transfer, quench_liquid_heat=quench_liquid_heat)


STIFFNESS = 1.0
EXPANSION = 0.6
SOFTENING_SCALE = 0.25
TIME_STEP = 0.4
DAMPING = 0.05
HEAT_INCREMENT = 1.0
GAP_GAIN = 0.5


def softening(opening):
    stretch = jnp.maximum(opening, 0.0)
    return 1.0 - jnp.exp(-stretch * stretch / SOFTENING_SCALE)


def edge_masks(row_first, col_first, height_number_all, width_number, total_rows, total_cols):
    row_index = row_first + jnp.arange(height_number_all, dtype=jnp.int32)
    col_index = col_first + jnp.arange(width_number, dtype=jnp.int32)
    in_rows = (row_index >= 0) & (row_index < total_rows)
    in_cols = (col_index >= 0) & (col_index < total_cols)
    present_horizontal = ((row_index >= 1) & (row_index < total_rows))[:, None] & in_cols[None, :]
    present_vertical = in_rows[:, None] & ((col_index >= 1) & (col_index < total_cols))[None, :]
    return present_horizontal.astype(jnp.float32), present_vertical.astype(jnp.float32)


def march_forward(state_tensors, dense_mesh_heat, present_horizontal, present_vertical):
    disp_x, disp_y, vel_x, vel_y, dam_x, dam_y, weight = [state_tensors[number] for number in range(7)]
    average_horizontal = 0.5 * (dense_mesh_heat[1:, :] + dense_mesh_heat[:-1, :])
    open_x = disp_x[1:, :] - disp_x[:-1, :] - EXPANSION * average_horizontal
    shear_x = disp_y[1:, :] - disp_y[:-1, :]
    new_dx = jnp.maximum(dam_x[1:, :], softening(open_x) * weight[1:, :] * present_horizontal[1:, :])
    spring_x = STIFFNESS * (1.0 - new_dx) * present_horizontal[1:, :]
    normal_x = spring_x * open_x
    along_x = spring_x * shear_x
    average_vertical = 0.5 * (dense_mesh_heat[:, 1:] + dense_mesh_heat[:, :-1])
    open_y = disp_y[:, 1:] - disp_y[:, :-1] - EXPANSION * average_vertical
    shear_y = disp_x[:, 1:] - disp_x[:, :-1]
    new_dy = jnp.maximum(dam_y[:, 1:], softening(open_y) * weight[:, 1:] * present_vertical[:, 1:])
    spring_y = STIFFNESS * (1.0 - new_dy) * present_vertical[:, 1:]
    normal_y = spring_y * open_y
    along_y = spring_y * shear_y
    force_x = (normal_x[1:, 1:-1] - normal_x[:-1, 1:-1]) + (along_y[1:-1, 1:] - along_y[1:-1, :-1])
    force_y = (along_x[1:, 1:-1] - along_x[:-1, 1:-1]) + (normal_y[1:-1, 1:] - normal_y[1:-1, :-1])
    inner_vx = vel_x[1:-1, 1:-1]
    inner_vy = vel_y[1:-1, 1:-1]
    next_vx = inner_vx + TIME_STEP * (force_x - DAMPING * inner_vx)
    next_vy = inner_vy + TIME_STEP * (force_y - DAMPING * inner_vy)
    next_ux = disp_x[1:-1, 1:-1] + TIME_STEP * next_vx
    next_uy = disp_y[1:-1, 1:-1] + TIME_STEP * next_vy
    return jnp.stack([next_ux, next_uy, next_vx, next_vy, new_dx[:-1, 1:-1], new_dy[1:-1, :-1], weight[1:-1, 1:-1]])


def widen_upward(padded):
    middle = padded[1:-1]
    even_rows = 0.75 * middle + 0.25 * padded[:-2]
    odd_rows = 0.75 * middle + 0.25 * padded[2:]
    return jnp.stack([even_rows, odd_rows], axis=1).reshape(2 * middle.shape[0], padded.shape[1])


def widen_sideways(padded):
    middle = padded[:, 1:-1]
    even_cols = 0.75 * middle + 0.25 * padded[:, :-2]
    odd_cols = 0.75 * middle + 0.25 * padded[:, 2:]
    return jnp.stack([even_cols, odd_cols], axis=2).reshape(padded.shape[0], 2 * middle.shape[1])


def kernel_table():
    position = jnp.arange(SEG, dtype=jnp.float32)
    return jnp.exp(-4.0 * jnp.abs(position[:, None] - position[None, :]) / SEG) * (2.0 / SEG)


def radiate(values):
    flattened = values.reshape(-1, SEG)
    product = jnp.dot(flattened, kernel_table(), precision=lax.Precision.HIGHEST, preferred_element_type=jnp.float32)
    return product.reshape(values.shape)


def sweep_plate(state_tensors, dense_margin, mask_x, mask_y):
    padded = jnp.pad(state_tensors, ((0, 0), (1, 1), (1, 1)))

    def one_block(block_index):
        first_row = (block_index * FX).astype(jnp.int32)
        piece_rows = lax.dynamic_slice_in_dim(padded, first_row, FX + 2, 1)
        warmth_lines = lax.dynamic_slice_in_dim(dense_margin, first_row, FX + 2, 0)
        rows_x = lax.dynamic_slice_in_dim(mask_x, first_row, FX + 2, 0)
        rows_y = lax.dynamic_slice_in_dim(mask_y, first_row, FX + 2, 0)
        return march_forward(piece_rows, warmth_lines, rows_x, rows_y)

    blocks = lax.map(one_block, jnp.arange(N_GX, dtype=jnp.int32))
    return jnp.moveaxis(blocks, 0, 1).reshape(7, NXF, NYF)


def heat_baseline_check(cell_warmth, heat_storage, surface_transfer, quench_liquid_heat, thermal_impedance):
    heat_conductance = (1.0 + 0.5 * cell_warmth) / (1.0 + thermal_impedance)
    padded_cond = jnp.pad(heat_conductance, 1)
    row_index = jnp.arange(CELL_HEIGHT_NUM, dtype=jnp.int32)[:, None]
    col_index = jnp.arange(CELL_WIDTH_NUM, dtype=jnp.int32)[None, :]
    cond_down = 0.5 * (heat_conductance + padded_cond[:-2, 1:-1]) * (row_index >= 1).astype(jnp.float32)
    cond_up = 0.5 * (heat_conductance + padded_cond[2:, 1:-1]) * (row_index <= CELL_HEIGHT_NUM - 2).astype(jnp.float32)
    cond_left = 0.5 * (heat_conductance + padded_cond[1:-1, :-2]) * (col_index >= 1).astype(jnp.float32)
    cond_right = 0.5 * (heat_conductance + padded_cond[1:-1, 2:]) * (col_index <= CELL_WIDTH_NUM - 2).astype(jnp.float32)
    offsum = cond_down + cond_up + cond_left + cond_right
    diagonal = (heat_storage / HEAT_INCREMENT + surface_transfer) + offsum
    off_ratio = offsum / diagonal
    bound_low = jnp.min(1.0 - off_ratio)
    bound_high = jnp.max(1.0 + off_ratio)

    def laplace_action(field):
        padded = jnp.pad(field, 1)
        return diagonal * field - (cond_down * padded[:-2, 1:-1] + cond_up * padded[2:, 1:-1]
                                   + cond_left * padded[1:-1, :-2] + cond_right * padded[1:-1, 2:])

    center = 0.5 * (bound_high + bound_low)
    spread = 0.5 * (bound_high - bound_low)
    sigma_ratio = center / spread
    rho_now = 1.0 / sigma_ratio
    forcing_entries = heat_storage / HEAT_INCREMENT * cell_warmth + surface_transfer * quench_liquid_heat
    misfit_norm = forcing_entries - laplace_action(cell_warmth)
    direction = misfit_norm / diagonal / center
    answer_state = cell_warmth
    for iteration in range(ITERS):
        answer_state = answer_state + direction
        if iteration + 1 < ITERS:
            misfit_norm = misfit_norm - laplace_action(direction)
            rho_next = 1.0 / (2.0 * sigma_ratio - rho_now)
            direction = rho_next * rho_now * direction + (2.0 * rho_next / spread) * (misfit_norm / diagonal)
            rho_now = rho_next
    return answer_state


def reference(node_shift, node_speed, damage_initial, cohesive_markers, cell_warmth, heat_storage, surface_transfer, quench_liquid_heat):
    weight = jnp.repeat(jnp.repeat(cohesive_markers, SR, axis=0), FY, axis=1).astype(jnp.float32)
    present_horizontal, present_vertical = edge_masks(0, 0, NXF, NYF, NXF, NYF)
    start_damage = damage_initial.astype(jnp.float32) * 0.125 * weight[None]
    state_tensors = jnp.stack([node_shift[0], node_shift[1], node_speed[0], node_speed[1],
                        start_damage[0] * present_horizontal, start_damage[1] * present_vertical, weight])
    dense_mesh_heat = widen_sideways(widen_upward(jnp.pad(cell_warmth, 1, mode="edge")))
    dense_margin = jnp.pad(dense_mesh_heat, 1)
    mask_x, mask_y = edge_masks(-1, -1, NXF + 2, NYF + 2, NXF, NYF)
    for substep in range(SUBSTEPS):
        state_tensors = sweep_plate(state_tensors, dense_margin, mask_x, mask_y)
    gap_sum = state_tensors[4] + state_tensors[5]
    glowing = radiate(gap_sum)
    thermal_impedance = GAP_GAIN * glowing.reshape(CELL_HEIGHT_NUM, 2, CELL_WIDTH_NUM, 2).sum(axis=(1, 3))
    warmth_after_solve = heat_baseline_check(cell_warmth, heat_storage, surface_transfer, quench_liquid_heat, thermal_impedance)
    return state_tensors[0:2], state_tensors[2:4], state_tensors[4:6].astype(jnp.bfloat16), warmth_after_solve
```

```python
import functools

import jax
import jax.numpy as jnp
from jax import lax
from jax.experimental import pallas as pl
from jax.experimental.pallas import tpu as pltpu
from jax.sharding import PartitionSpec as P

SR = 8
SEG = 128
SUBSTEPS = 8
HALO = 8
MESH = pl.DeviceIdType.MESH
F32 = jnp.float32


def lane_iota(shape):
    return lax.broadcasted_iota(jnp.int32, shape, 1)


def row_iota(shape):
    return lax.broadcasted_iota(jnp.int32, shape, 0)


def full_dot(a, b):
    return jnp.dot(a, b, precision=lax.Precision.HIGHEST, preferred_element_type=F32)


def kernel(
    n_gx,
    n_gy,
    shift,
    speed,
    level,
    mark,
    warm,
    store,
    film,
    bath,
    o_shift,
    o_speed,
    o_dam,
    o_warm,
    tsend,
    trecv,
    asend,
    arecv,
    pk_l,
    pk_r,
    rk_l,
    rk_r,
    rowsend,
    rowrecv,
    state,
    wt,
    tx,
    ty,
    tc,
    ac,
    fc,
    widebuf,
    gap,
    cbuf,
    crow,
    ccl,
    ccr,
    zsend,
    zrecv,
    msend,
    mrecv,
    nb_send,
    nb_recv,
    t_sem,
    a_sem,
    c_send,
    c_recv,
    z_sem,
    m_sem,
):
    ndev = n_gx * n_gy
    gx = lax.axis_index("gx")
    gy = lax.axis_index("gy")
    me = gx * n_gy + gy
    _, hh, ww = shift.shape
    rpd, _ = warm.shape
    cw = ww // 2
    ch = hh // 2
    hb = HALO // rpd
    nsl = n_gy + 2 * hb
    up = lax.rem(gx + n_gx - 1, n_gx)
    down = lax.rem(gx + 1, n_gx)
    left = lax.rem(gy + n_gy - 1, n_gy)
    right = lax.rem(gy + 1, n_gy)

    barrier = pltpu.get_barrier_semaphore()

    def greet(k, c):
        t = lax.rem(me + k, ndev)
        pl.semaphore_signal(barrier, inc=1, device_id=(t // n_gy, t % n_gy), device_id_type=MESH)
        return c

    lax.fori_loop(1, ndev, greet, 0)

    lane = lane_iota((hh, 128))
    for s in range(hh // SR):
        w8 = jnp.broadcast_to(mark[s : s + 1, :].astype(F32), (SR, ww))
        wt[HALO + SR * s : HALO + SR * s + SR, 0:ww] = w8
    w_own = wt[HALO : HALO + hh, 0:ww]
    grow = gx * hh + row_iota((hh, ww))
    gcol = gy * ww + lane_iota((hh, ww))
    dam0 = jnp.where(grow >= 1, level[0].astype(F32) * 0.125 * w_own, 1.0)
    dam1 = jnp.where(gcol >= 1, level[1].astype(F32) * 0.125 * w_own, 1.0)
    own = [shift[0], shift[1], speed[0], speed[1], dam0, dam1]
    for f in range(6):
        state[f, HALO : HALO + hh, 0:ww] = own[f]
    acc_l = jnp.zeros((hh, 128), F32)
    acc_r = jnp.zeros((hh, 128), F32)
    for f, val in enumerate(own + [w_own]):
        first, last = val[:, 0:128], val[:, ww - 128 : ww]
        here = (lane >= 8 * f) & (lane < 8 * f + 8)
        first = pltpu.roll(first, 8 * f, 1) if f else first
        acc_l = jnp.where(here, first, acc_l)
        acc_r = jnp.where(here, pltpu.roll(last, 8 * f + 8, 1), acc_r)
        if f < 6:
            rowsend[0, :, ww * f : ww * f + ww] = val[0:8, :]
            rowsend[1, :, ww * f : ww * f + ww] = val[hh - 8 : hh, :]
        else:
            rowsend[0, :, ww * f : ww * f + 128] = val[0:8, 0:128]
            rowsend[1, :, ww * f : ww * f + 128] = val[hh - 8 : hh, 0:128]
    pk_l[...] = acc_l
    pk_r[...] = acc_r

    lane_c = lane_iota((rpd, 128))

    def chunk(value, k):
        after = value[:, (cw * (k + 1)) % (cw * n_gy) :][:, 0:128]
        before = value[:, (cw * k - 128) % (cw * n_gy) :][:, 0:128]
        return value[:, cw * k : cw * k + cw], jnp.where(lane_c < 64, after, before)

    t_own = warm[...]
    base = store[...] + film[...]
    force_own = store[...] * t_own + film[...] * bath[...]
    for k in range(n_gy):
        main, edge = chunk(t_own, k)
        tsend[k, :, 0:cw] = main
        tsend[k, :, cw : cw + 128] = edge
        for q, val in enumerate((base, force_own)):
            main, edge = chunk(val, k)
            asend[k, q, :, 0:cw] = main
            asend[k, q, :, cw : cw + 128] = edge

    pl.semaphore_wait(barrier, ndev - 1)

    def remote(src, dst, ssem, rsem, where):
        return pltpu.make_async_remote_copy(
            src_ref=src, dst_ref=dst, send_sem=ssem, recv_sem=rsem, device_id=where,
            device_id_type=MESH,
        )

    def neighbours(send_l, send_r, row_u, row_d, recv_l, recv_r, got, rows, ssem, rsem):
        top, end = slice(0, 8), slice(rows - 8, rows)
        lo, mid, hi = slice(0, 8), slice(8, rows + 8), slice(rows + 8, rows + 16)
        return [
            remote(row_u, got.at[1], ssem.at[0], rsem.at[0], (up, gy)),
            remote(row_d, got.at[0], ssem.at[1], rsem.at[1], (down, gy)),
            remote(send_l, recv_r.at[mid], ssem.at[2], rsem.at[2], (gx, left)),
            remote(send_r, recv_l.at[mid], ssem.at[3], rsem.at[3], (gx, right)),
            remote(send_l.at[top], recv_r.at[hi], ssem.at[4], rsem.at[4], (up, left)),
            remote(send_r.at[top], recv_l.at[hi], ssem.at[5], rsem.at[5], (up, right)),
            remote(send_l.at[end], recv_r.at[lo], ssem.at[6], rsem.at[6], (down, left)),
            remote(send_r.at[end], recv_l.at[lo], ssem.at[7], rsem.at[7], (down, right)),
        ]

    first = neighbours(
        pk_l, pk_r, rowsend.at[0], rowsend.at[1], rk_l, rk_r, rowrecv, hh, nb_send, nb_recv
    )

    def spread_out(send, recv, sem):
        def along(k, c):
            t = lax.rem(gy + k, n_gy)
            remote(send.at[t], recv.at[gy + hb], sem.at[1], sem.at[0], (gx, t)).start()
            return c

        lax.fori_loop(1, n_gy, along, 0)
        pltpu.make_async_copy(send.at[gy], recv.at[gy + hb], sem.at[0]).start()

        @pl.when(gy < hb)
        def _():
            def go(k, c):
                remote(
                    send.at[k], recv.at[gy + hb + n_gy], sem.at[2], sem.at[0], (up, k)
                ).start()
                return c

            lax.fori_loop(0, n_gy, go, 0)

        @pl.when(gy >= n_gy - hb)
        def _():
            def go(k, c):
                remote(
                    send.at[k], recv.at[gy - (n_gy - hb)], sem.at[3], sem.at[0], (down, k)
                ).start()
                return c

            lax.fori_loop(0, n_gy, go, 0)

    def spread_sent(send, recv, sem):
        part = pl.ds(0, n_gy - 1)
        remote(send.at[part], recv.at[part], sem.at[1], sem.at[0], (gx, right)).wait_send()
        whole = pl.ds(0, n_gy)

        @pl.when(gy < hb)
        def _():
            remote(send, recv.at[whole], sem.at[2], sem.at[0], (up, gy)).wait_send()

        @pl.when(gy >= n_gy - hb)
        def _():
            remote(send, recv.at[whole], sem.at[3], sem.at[0], (down, gy)).wait_send()

    spread_out(tsend, trecv, t_sem)
    for copy in first:
        copy.start()
    spread_out(asend, arecv, a_sem)

    pltpu.make_async_copy(trecv, trecv, t_sem.at[0]).wait()
    crows = ch + 16
    for k in range(nsl):
        tc[rpd * k : rpd * k + rpd, :] = trecv[k]
    cshape = (crows, cw + 128)
    crow_i, clane_i = row_iota(cshape), lane_iota(cshape)
    t_all = tc[...]
    p = t_all
    p = jnp.where((gx == 0) & (crow_i < 8), t_all[8:9, :], p)
    p = jnp.where((gx == n_gx - 1) & (crow_i >= ch + 8), t_all[ch + 7 : ch + 8, :], p)
    wide = cw + 128
    q = jnp.where((gy == 0) & (clane_i == wide - 1), pltpu.roll(p, wide - 1, 1), p)
    q = jnp.where((gy == n_gy - 1) & (clane_i == cw), pltpu.roll(p, 1, 1), q)
    even = 0.75 * q + 0.25 * pltpu.roll(q, 1, 0)
    odd = 0.75 * q + 0.25 * pltpu.roll(q, crows - 1, 0)
    frows = hh + 2 * HALO
    need = frows // 2
    ntile = wide // 128
    for t in range(ntile):
        cols = slice(128 * t, 128 * t + 128)
        widebuf[t, pl.ds(0, need, stride=2), :] = even[4 : 4 + need, cols]
        widebuf[t, pl.ds(1, need, stride=2), :] = odd[4 : 4 + need, cols]
    r = jnp.concatenate([widebuf[t] for t in range(ntile)], axis=1)
    ecol = 0.75 * r + 0.25 * pltpu.roll(r, 1, 1)
    ocol = 0.75 * r + 0.25 * pltpu.roll(r, wide - 1, 1)
    k_i, n_i = row_iota((256, 256)), lane_iota((256, 256))
    weave = (n_i == jnp.where(k_i < 128, 2 * k_i, 2 * k_i - 255)).astype(F32)
    stack = jnp.concatenate(
        [
            jnp.concatenate([ecol[:, 128 * t : 128 * t + 128], ocol[:, 128 * t : 128 * t + 128]], 1)
            for t in range(ntile)
        ],
        axis=0,
    )
    woven = full_dot(stack, weave)
    lane_f = lane_iota((frows, 128))
    pieces = [woven[frows * t : frows * t + frows] for t in range(ntile)]
    edge = jnp.where(lane_f < 64, pieces[-1][:, 0:128], pieces[-1][:, 128:256])
    fine = jnp.concatenate(pieces[:-1] + [edge], axis=1)
    fwide = ww + 128
    tx[...] = 0.6 * (0.5 * (fine + pltpu.roll(fine, 1, 0)))
    ty[...] = 0.6 * (0.5 * (fine + pltpu.roll(fine, 1, 1)))

    for copy in first:
        copy.wait_recv()
    got_l, got_r = rk_l[...], rk_r[...]
    for f in range(7):
        from_r = pltpu.roll(got_r, 128 - 8 * f, 1) if f else got_r
        from_l = pltpu.roll(got_l, 120 - 8 * f, 1)
        side = jnp.where(lane_f < 8, from_r, jnp.where(lane_f >= 120, from_l, 0.0))
        if f == 5:
            off_l = (gy == 0) & (lane_f >= 64)
            off_r = (gy == n_gy - 1) & (lane_f < 64)
            side = jnp.where(off_l | off_r, 1.0, side)
        target = state.at[f] if f < 6 else wt
        target[:, ww:fwide] = side
        for side_row, at in ((0, 0), (1, hh + HALO)):
            if f < 6:
                target[at : at + 8, 0:ww] = rowrecv[side_row, :, ww * f : ww * f + ww]
            else:
                part = rowrecv[side_row, :, ww * f : ww * f + 128]
                for t in range(ww // 128):
                    target[at : at + 8, 128 * t : 128 * t + 128] = part

    @pl.when(gx == 0)
    def _():
        state[4, 0:8, :] = jnp.ones((8, fwide), F32)

    @pl.when(gx == n_gx - 1)
    def _():
        state[4, hh + HALO : hh + HALO + 8, :] = jnp.ones((8, fwide), F32)

    sub = row_iota((8, fwide))

    def substep(_, c):
        old = None
        for s in range(frows // 8 + 1):
            if s < frows // 8:
                rows = slice(8 * s, 8 * s + 8)
                u0, u1 = state[0, rows, :], state[1, rows, :]
                w = wt[rows, :]
                r0, r1 = pltpu.roll(u0, 1, 0), pltpu.roll(u1, 1, 0)
                p0 = jnp.where(sub == 0, old["r0"], r0) if old else r0
                p1 = jnp.where(sub == 0, old["r1"], r1) if old else r1
                open_x = u0 - p0 - tx[rows, :]
                st = jnp.maximum(open_x, 0.0)
                dx = jnp.maximum(state[4, rows, :], (1.0 - jnp.exp(st * st * -4.0)) * w)
                state[4, rows, :] = dx
                sp = 1.0 - dx
                nx = sp * open_x
                ax = sp * (u1 - p1)
                open_y = u1 - pltpu.roll(u1, 1, 1) - ty[rows, :]
                st = jnp.maximum(open_y, 0.0)
                dy = jnp.maximum(state[5, rows, :], (1.0 - jnp.exp(st * st * -4.0)) * w)
                state[5, rows, :] = dy
                sp = 1.0 - dy
                ny = sp * open_y
                ay = sp * (u0 - pltpu.roll(u0, 1, 1))
                new = dict(
                    r0=r0, r1=r1, nx=nx, ax=ax, u0=u0, u1=u1,
                    sx=pltpu.roll(nx, 7, 0), sa=pltpu.roll(ax, 7, 0),
                    fy0=pltpu.roll(ay, fwide - 1, 1) - ay,
                    fy1=pltpu.roll(ny, fwide - 1, 1) - ny,
                )
            if old:
                rows = slice(8 * s - 8, 8 * s)
                nn = jnp.where(sub == 7, new["sx"], old["sx"])
                na = jnp.where(sub == 7, new["sa"], old["sa"])
                f0 = (nn - old["nx"]) + old["fy0"]
                f1 = (na - old["ax"]) + old["fy1"]
                v0, v1 = state[2, rows, :], state[3, rows, :]
                v0 = v0 + 0.4 * (f0 - 0.05 * v0)
                v1 = v1 + 0.4 * (f1 - 0.05 * v1)
                state[2, rows, :] = v0
                state[3, rows, :] = v1
                state[0, rows, :] = old["u0"] + 0.4 * v0
                state[1, rows, :] = old["u1"] + 0.4 * v1
            old = new
        return c

    lax.fori_loop(0, SUBSTEPS, substep, 0)

    own_r = slice(HALO, HALO + hh)
    dam_x = jnp.where(grow >= 1, state[4, own_r, 0:ww], 0.0)
    dam_y = jnp.where(gcol >= 1, state[5, own_r, 0:ww], 0.0)
    both = dam_x + dam_y
    for t in range(ww // 128):
        gap[t] = both[:, 128 * t : 128 * t + 128]
    rows2 = jnp.concatenate(
        [
            gap[t, pl.ds(0, ch, stride=2), :] + gap[t, pl.ds(1, ch, stride=2), :]
            for t in range(ww // 128)
        ],
        axis=1,
    )
    k_i, n_i = row_iota((256, 128)), lane_iota((256, 128))
    pos = (k_i % SEG).astype(F32)
    col = (2 * (n_i % 64)).astype(F32)
    tab = jnp.exp(jnp.abs(pos - col) * (-4.0 / SEG)) + jnp.exp(jnp.abs(pos - col - 1.0) * (-4.0 / SEG))
    tab = jnp.where(k_i // SEG == n_i // 64, tab * (1.0 / SEG), 0.0)
    npair = ww // 256
    glow = full_dot(
        jnp.concatenate([rows2[:, 256 * t : 256 * t + 256] for t in range(npair)], axis=0), tab
    )
    resist = jnp.concatenate([glow[ch * t : ch * t + ch] for t in range(npair)], axis=1)
    cond_own = (1.0 + 0.5 * tc[8 : 8 + ch, 0:cw]) / (1.0 + resist)
    cbuf[...] = cond_own
    second = neighbours(
        cbuf.at[:, 0:128], cbuf.at[:, cw - 128 : cw], cbuf.at[0:8], cbuf.at[ch - 8 : ch],
        ccl, ccr, crow, ch, c_send, c_recv,
    )
    for copy in second:
        copy.start()

    o_shift[0] = state[0, own_r, 0:ww]
    o_shift[1] = state[1, own_r, 0:ww]
    o_speed[0] = state[2, own_r, 0:ww]
    o_speed[1] = state[3, own_r, 0:ww]
    o_dam[0] = dam_x.astype(jnp.bfloat16)
    o_dam[1] = dam_y.astype(jnp.bfloat16)

    pltpu.make_async_copy(arecv, arecv, a_sem.at[0]).wait()
    for k in range(nsl):
        ac[rpd * k : rpd * k + rpd, :] = arecv[k, 0]
        fc[rpd * k : rpd * k + rpd, :] = arecv[k, 1]

    for copy in second:
        copy.wait_recv()
    lane_k = lane_iota((crows, 128))
    cond = jnp.concatenate(
        [
            jnp.concatenate([crow[0], cbuf[...], crow[1]], axis=0),
            jnp.where(lane_k < 64, ccr[...], ccl[...]),
        ],
        axis=1,
    )
    crow_g = gx * ch - 8 + crow_i
    ccol_g = gy * cw + jnp.where(clane_i < cw + 64, clane_i, clane_i - wide)

    def four(x):
        return (
            pltpu.roll(x, 1, 0),
            pltpu.roll(x, crows - 1, 0),
            pltpu.roll(x, 1, 1),
            pltpu.roll(x, wide - 1, 1),
        )

    masks = (
        crow_g >= 1,
        crow_g <= ch * n_gx - 2,
        ccol_g >= 1,
        ccol_g <= cw * n_gy - 2,
    )
    faces = [
        jnp.where(m, 0.5 * (cond + nb), 0.0) for m, nb in zip(masks, four(cond))
    ]
    offsum = faces[0] + faces[1] + faces[2] + faces[3]
    diagonal = ac[...] + offsum
    ratio = offsum / diagonal
    peak = jnp.max(ratio[8 : 8 + ch, 0:cw])
    msend[...] = jnp.full((8, 128), peak, F32)

    def tell(k, c):
        t = lax.rem(me + k, ndev)
        remote(
            msend, mrecv.at[k - 1], m_sem.at[1], m_sem.at[0], (t // n_gy, t % n_gy)
        ).start()
        return c

    lax.fori_loop(1, ndev, tell, 0)

    t_all = tc[...]
    near = sum(f * nb for f, nb in zip(faces, four(t_all)))
    z = (fc[...] - (diagonal * t_all - near)) / diagonal
    faces = [f / diagonal for f in faces]
    for j in range(4):
        if j:
            z = z - sum(f * nb for f, nb in zip(faces, four(z)))
        for k in range(n_gy):
            zsend[k, j] = z[8 + rpd * k : 8 + rpd * k + rpd, 0:cw]

    def home(k, c):
        t = lax.rem(gy + k, n_gy)
        remote(zsend.at[t], zrecv.at[gy], z_sem.at[1], z_sem.at[0], (gx, t)).start()
        return c

    lax.fori_loop(1, n_gy, home, 0)
    pltpu.make_async_copy(zsend.at[gy], zrecv.at[gy], z_sem.at[0]).start()

    pltpu.make_async_copy(mrecv, mrecv, m_sem.at[0]).wait()
    peak = jnp.maximum(jnp.max(mrecv[...], axis=0), msend[...])[0:1, :]
    low, high = 1.0 - peak, 1.0 + peak
    center = 0.5 * (high + low)
    spread = 0.5 * (high - low)
    sigma = center / spread
    rho = 1.0 / sigma
    zero = jnp.zeros_like(center)
    e = [zero + 1.0, zero, zero, zero]
    d = [1.0 / center, zero, zero, zero]
    total = list(d)
    for _ in range(3):
        e = [e[0]] + [e[i] - d[i - 1] for i in range(1, 4)]
        rho_next = 1.0 / (2.0 * sigma - rho)
        d = [rho_next * rho * d[i] + (2.0 * rho_next / spread) * e[i] for i in range(4)]
        total = [a + b for a, b in zip(total, d)]
        rho = rho_next
    total = [jnp.concatenate([c] * (cw // 128), axis=1) for c in total]

    pltpu.make_async_copy(zrecv, zrecv, z_sem.at[0]).wait()
    for k in range(n_gy):
        x = warm[:, cw * k : cw * k + cw]
        for j in range(4):
            x = x + total[j] * zrecv[k, j]
        o_warm[:, cw * k : cw * k + cw] = x

    for copy in first + second:
        copy.wait_send()
    spread_sent(tsend, trecv, t_sem)
    spread_sent(asend, arecv, a_sem)
    part = pl.ds(0, n_gy - 1)
    remote(zsend.at[part], zrecv.at[part], z_sem.at[1], z_sem.at[0], (gx, right)).wait_send()
    remote(mrecv, mrecv, m_sem.at[1], m_sem.at[0], (gx, right)).wait_send()


def per_device(n_gx, n_gy, shift, speed, level, mark, warm, store, film, bath):
    _, hh, ww = shift.shape
    rpd, _ = warm.shape
    cw, ch = ww // 2, hh // 2
    wide, fwide = cw + 128, ww + 128
    crows, frows = ch + 16, hh + 2 * HALO
    nsl = n_gy + 2 * (HALO // rpd)
    vm = lambda *s: pltpu.VMEM(s, F32)
    dma = lambda n: pltpu.SemaphoreType.DMA((n,))
    spec = pl.BlockSpec(memory_space=pltpu.VMEM)
    return pl.pallas_call(
        functools.partial(kernel, n_gx, n_gy),
        out_shape=(
            jax.ShapeDtypeStruct(shift.shape, F32),
            jax.ShapeDtypeStruct(speed.shape, F32),
            jax.ShapeDtypeStruct(level.shape, jnp.bfloat16),
            jax.ShapeDtypeStruct(warm.shape, F32),
        ),
        in_specs=[spec] * 8,
        out_specs=(spec,) * 4,
        scratch_shapes=[
            vm(n_gy, rpd, wide),
            vm(nsl, rpd, wide),
            vm(n_gy, 2, rpd, wide),
            vm(nsl, 2, rpd, wide),
            vm(hh, 128),
            vm(hh, 128),
            vm(frows, 128),
            vm(frows, 128),
            vm(2, 8, 6 * ww + 128),
            vm(2, 8, 6 * ww + 128),
            vm(6, frows, fwide),
            vm(frows, fwide),
            vm(frows, fwide),
            vm(frows, fwide),
            vm(crows, wide),
            vm(crows, wide),
            vm(crows, wide),
            vm(wide // 128, frows, 128),
            vm(ww // 128, hh, 128),
            vm(ch, cw),
            vm(2, 8, cw),
            vm(crows, 128),
            vm(crows, 128),
            vm(n_gy, 4, rpd, cw),
            vm(n_gy, 4, rpd, cw),
            vm(8, 128),
            vm(n_gx * n_gy - 1, 8, 128),
            dma(8),
            dma(8),
            dma(4),
            dma(4),
            dma(8),
            dma(8),
            dma(2),
            dma(2),
        ],
        compiler_params=pltpu.CompilerParams(
            collective_id=0, has_side_effects=True, vmem_limit_bytes=32 * 1024 * 1024
        ),
    )(shift, speed, level, mark, warm, store, film, bath)


def solution(mesh):
    rows = P(("gx", "gy"), None)
    plate = P(None, "gx", "gy")
    return jax.shard_map(
        functools.partial(per_device, mesh.shape["gx"], mesh.shape["gy"]),
        mesh=mesh,
        in_specs=(plate, plate, plate, P("gx", "gy"), rows, rows, rows, rows),
        out_specs=(plate, plate, plate, rows),
        check_vma=False,
    )
```

```python
import functools

import jax
import jax.numpy as jnp
from jax import lax
from jax.experimental import pallas as pl
from jax.experimental.pallas import tpu as pltpu
from jax.sharding import PartitionSpec as P

SR = 8
SEG = 128
SUBSTEPS = 8
HALO = 8
MESH = pl.DeviceIdType.MESH
F32 = jnp.float32


def lane_iota(shape):
    return lax.broadcasted_iota(jnp.int32, shape, 1)


def row_iota(shape):
    return lax.broadcasted_iota(jnp.int32, shape, 0)


def full_dot(a, b):
    return jnp.dot(a, b, precision=lax.Precision.HIGHEST, preferred_element_type=F32)


def kernel(
    n_gx,
    n_gy,
    shift,
    speed,
    level_h,
    mark,
    warm_h,
    store_h,
    film_h,
    bath_h,
    o_shift,
    o_speed,
    o_dam,
    o_warm,
    tsend,
    trecv,
    asend,
    arecv,
    pk_l,
    pk_r,
    rk_l,
    rk_r,
    wsend,
    wrecv,
    level,
    warm,
    store,
    film,
    bath,
    state,
    wt,
    tx,
    ty,
    tc,
    ac,
    fc,
    widebuf,
    gap,
    cbuf,
    crow,
    ccl,
    ccr,
    zsend,
    zrecv,
    msend,
    mrecv,
    nb_send,
    nb_recv,
    t_sem,
    a_sem,
    c_send,
    c_recv,
    z_sem,
    m_sem,
    in_sem,
    dambuf,
    warmbuf,
    out_sem,
):
    ndev = n_gx * n_gy
    gx = lax.axis_index("gx")
    gy = lax.axis_index("gy")
    me = gx * n_gy + gy
    _, hh, ww = shift.shape
    rpd, _ = warm_h.shape
    cw = ww // 2
    ch = hh // 2
    hb = HALO // rpd
    nsl = n_gy + 2 * hb
    up = lax.rem(gx + n_gx - 1, n_gx)
    down = lax.rem(gx + 1, n_gx)
    left = lax.rem(gy + n_gy - 1, n_gy)
    right = lax.rem(gy + 1, n_gy)

    own_r = slice(HALO, HALO + hh)
    loads = [
        pltpu.make_async_copy(src, dst, in_sem.at[i])
        for i, (src, dst) in enumerate(
            (
                (warm_h, warm),
                (level_h, level),
                (shift, state.at[0:2, own_r, 0:ww]),
                (speed, state.at[2:4, own_r, 0:ww]),
                (store_h, store),
                (film_h, film),
                (bath_h, bath),
            )
        )
    ]
    for copy in loads:
        copy.start()
    barrier = pltpu.get_barrier_semaphore()

    def greet(k, c):
        t = lax.rem(me + k, ndev)
        pl.semaphore_signal(barrier, inc=1, device_id=(t // n_gy, t % n_gy), device_id_type=MESH)
        return c

    lax.fori_loop(1, ndev, greet, 0)

    lane = lane_iota((hh, 128))
    for s in range(hh // SR):
        wt[HALO + SR * s : HALO + SR * s + SR, 0:ww] = jnp.full((SR, ww), mark[0, s], jnp.int32).astype(F32)
    w_own = wt[own_r, 0:ww]
    grow = gx * hh + row_iota((hh, ww))
    gcol = gy * ww + lane_iota((hh, ww))
    loads[1].wait()
    state[4, own_r, 0:ww] = jnp.where(grow >= 1, level[0].astype(F32) * 0.125 * w_own, 1.0)
    state[5, own_r, 0:ww] = jnp.where(gcol >= 1, level[1].astype(F32) * 0.125 * w_own, 1.0)
    wsend[0] = wt[HALO : HALO + 8, 0:128]
    wsend[1] = wt[HALO + hh - 8 : HALO + hh, 0:128]
    loads[2].wait()
    loads[3].wait()
    acc_l = jnp.zeros((hh, 128), F32)
    acc_r = jnp.zeros((hh, 128), F32)
    for f in range(7):
        field = state.at[f] if f < 6 else wt
        first, last = field[own_r, 0:128], field[own_r, ww - 128 : ww]
        here = (lane >= 8 * f) & (lane < 8 * f + 8)
        first = pltpu.roll(first, 8 * f, 1) if f else first
        acc_l = jnp.where(here, first, acc_l)
        acc_r = jnp.where(here, pltpu.roll(last, 8 * f + 8, 1), acc_r)
    pk_l[...] = acc_l
    pk_r[...] = acc_r

    lane_c = lane_iota((rpd, 128))

    def chunk(value, k):
        after = value[:, (cw * (k + 1)) % (cw * n_gy) :][:, 0:128]
        before = value[:, (cw * k - 128) % (cw * n_gy) :][:, 0:128]
        return value[:, cw * k : cw * k + cw], jnp.where(lane_c < 64, after, before)

    for i in (0, 4, 5, 6):
        loads[i].wait()
    t_own = warm[...]
    base = store[...] + film[...]
    force_own = store[...] * t_own + film[...] * bath[...]
    for k in range(n_gy):
        main, edge = chunk(t_own, k)
        tsend[k, :, 0:cw] = main
        tsend[k, :, cw : cw + 128] = edge
        for q, val in enumerate((base, force_own)):
            main, edge = chunk(val, k)
            asend[k, q, :, 0:cw] = main
            asend[k, q, :, cw : cw + 128] = edge

    pl.semaphore_wait(barrier, ndev - 1)

    def remote(src, dst, ssem, rsem, where):
        return pltpu.make_async_remote_copy(
            src_ref=src, dst_ref=dst, send_sem=ssem, recv_sem=rsem, device_id=where,
            device_id_type=MESH,
        )

    def neighbours(send_l, send_r, row_u, row_d, recv_l, recv_r, got_u, got_d, rows, ssem, rsem):
        top, end = slice(0, 8), slice(rows - 8, rows)
        lo, mid, hi = slice(0, 8), slice(8, rows + 8), slice(rows + 8, rows + 16)
        return [
            remote(row_u, got_d, ssem.at[0], rsem.at[0], (up, gy)),
            remote(row_d, got_u, ssem.at[1], rsem.at[1], (down, gy)),
            remote(send_l, recv_r.at[mid], ssem.at[2], rsem.at[2], (gx, left)),
            remote(send_r, recv_l.at[mid], ssem.at[3], rsem.at[3], (gx, right)),
            remote(send_l.at[top], recv_r.at[hi], ssem.at[4], rsem.at[4], (up, left)),
            remote(send_r.at[top], recv_l.at[hi], ssem.at[5], rsem.at[5], (up, right)),
            remote(send_l.at[end], recv_r.at[lo], ssem.at[6], rsem.at[6], (down, left)),
            remote(send_r.at[end], recv_l.at[lo], ssem.at[7], rsem.at[7], (down, right)),
        ]

    first = neighbours(
        pk_l,
        pk_r,
        state.at[:, HALO : HALO + 8, 0:ww],
        state.at[:, HALO + hh - 8 : HALO + hh, 0:ww],
        rk_l,
        rk_r,
        state.at[:, 0:8, 0:ww],
        state.at[:, HALO + hh : HALO + hh + 8, 0:ww],
        hh,
        nb_send,
        nb_recv,
    ) + [
        remote(wsend.at[0], wrecv.at[1], nb_send.at[8], nb_recv.at[8], (up, gy)),
        remote(wsend.at[1], wrecv.at[0], nb_send.at[9], nb_recv.at[9], (down, gy)),
    ]

    def spread_out(send, recv, sem):
        def along(k, c):
            t = lax.rem(gy + k, n_gy)
            remote(send.at[t], recv.at[gy + hb], sem.at[1], sem.at[0], (gx, t)).start()
            return c

        lax.fori_loop(1, n_gy, along, 0)
        pltpu.make_async_copy(send.at[gy], recv.at[gy + hb], sem.at[0]).start()

        @pl.when(gy < hb)
        def _():
            def go(k, c):
                remote(
                    send.at[k], recv.at[gy + hb + n_gy], sem.at[2], sem.at[0], (up, k)
                ).start()
                return c

            lax.fori_loop(0, n_gy, go, 0)

        @pl.when(gy >= n_gy - hb)
        def _():
            def go(k, c):
                remote(
                    send.at[k], recv.at[gy - (n_gy - hb)], sem.at[3], sem.at[0], (down, k)
                ).start()
                return c

            lax.fori_loop(0, n_gy, go, 0)

    def spread_sent(send, recv, sem):
        part = pl.ds(0, n_gy - 1)
        remote(send.at[part], recv.at[part], sem.at[1], sem.at[0], (gx, right)).wait_send()
        whole = pl.ds(0, n_gy)

        @pl.when(gy < hb)
        def _():
            remote(send, recv.at[whole], sem.at[2], sem.at[0], (up, gy)).wait_send()

        @pl.when(gy >= n_gy - hb)
        def _():
            remote(send, recv.at[whole], sem.at[3], sem.at[0], (down, gy)).wait_send()

    spread_out(tsend, trecv, t_sem)
    for copy in first:
        copy.start()
    spread_out(asend, arecv, a_sem)

    pltpu.make_async_copy(trecv, trecv, t_sem.at[0]).wait()
    crows = ch + 16
    for k in range(nsl):
        tc[rpd * k : rpd * k + rpd, :] = trecv[k]
    cshape = (crows, cw + 128)
    crow_i, clane_i = row_iota(cshape), lane_iota(cshape)
    t_all = tc[...]
    p = t_all
    p = jnp.where((gx == 0) & (crow_i < 8), t_all[8:9, :], p)
    p = jnp.where((gx == n_gx - 1) & (crow_i >= ch + 8), t_all[ch + 7 : ch + 8, :], p)
    wide = cw + 128
    q = jnp.where((gy == 0) & (clane_i == wide - 1), pltpu.roll(p, wide - 1, 1), p)
    q = jnp.where((gy == n_gy - 1) & (clane_i == cw), pltpu.roll(p, 1, 1), q)
    even = 0.75 * q + 0.25 * pltpu.roll(q, 1, 0)
    odd = 0.75 * q + 0.25 * pltpu.roll(q, crows - 1, 0)
    frows = hh + 2 * HALO
    need = frows // 2
    ntile = wide // 128
    for t in range(ntile):
        cols = slice(128 * t, 128 * t + 128)
        widebuf[t, pl.ds(0, need, stride=2), :] = even[4 : 4 + need, cols]
        widebuf[t, pl.ds(1, need, stride=2), :] = odd[4 : 4 + need, cols]
    r = jnp.concatenate([widebuf[t] for t in range(ntile)], axis=1)
    ecol = 0.75 * r + 0.25 * pltpu.roll(r, 1, 1)
    ocol = 0.75 * r + 0.25 * pltpu.roll(r, wide - 1, 1)
    k_i, n_i = row_iota((256, 256)), lane_iota((256, 256))
    weave = (n_i == jnp.where(k_i < 128, 2 * k_i, 2 * k_i - 255)).astype(F32)
    stack = jnp.concatenate(
        [
            jnp.concatenate([ecol[:, 128 * t : 128 * t + 128], ocol[:, 128 * t : 128 * t + 128]], 1)
            for t in range(ntile)
        ],
        axis=0,
    )
    woven = full_dot(stack, weave)
    lane_f = lane_iota((frows, 128))
    pieces = [woven[frows * t : frows * t + frows] for t in range(ntile)]
    edge = jnp.where(lane_f < 64, pieces[-1][:, 0:128], pieces[-1][:, 128:256])
    fine = jnp.concatenate(pieces[:-1] + [edge], axis=1)
    fwide = ww + 128
    tx[...] = 0.6 * (0.5 * (fine + pltpu.roll(fine, 1, 0)))
    ty[...] = 0.6 * (0.5 * (fine + pltpu.roll(fine, 1, 1)))

    for copy in first:
        copy.wait_recv()
    got_l, got_r = rk_l[...], rk_r[...]
    for f in range(7):
        from_r = pltpu.roll(got_r, 128 - 8 * f, 1) if f else got_r
        from_l = pltpu.roll(got_l, 120 - 8 * f, 1)
        side = jnp.where(lane_f < 8, from_r, jnp.where(lane_f >= 120, from_l, 0.0))
        if f == 5:
            off_l = (gy == 0) & (lane_f >= 64)
            off_r = (gy == n_gy - 1) & (lane_f < 64)
            side = jnp.where(off_l | off_r, 1.0, side)
        target = state.at[f] if f < 6 else wt
        target[:, ww:fwide] = side
    for side_row, at in ((0, 0), (1, hh + HALO)):
        for t in range(ww // 128):
            wt[at : at + 8, 128 * t : 128 * t + 128] = wrecv[side_row]

    @pl.when(gx == 0)
    def _():
        state[4, 0:8, :] = jnp.ones((8, fwide), F32)

    @pl.when(gx == n_gx - 1)
    def _():
        state[4, hh + HALO : hh + HALO + 8, :] = jnp.ones((8, fwide), F32)

    for copy in first:
        copy.wait_send()

    sub = row_iota((8, fwide))

    def substep(_, c):
        old = None
        for s in range(frows // 8 + 1):
            if s < frows // 8:
                rows = slice(8 * s, 8 * s + 8)
                u0, u1 = state[0, rows, :], state[1, rows, :]
                w = wt[rows, :]
                r0, r1 = pltpu.roll(u0, 1, 0), pltpu.roll(u1, 1, 0)
                p0 = jnp.where(sub == 0, old["r0"], r0) if old else r0
                p1 = jnp.where(sub == 0, old["r1"], r1) if old else r1
                open_x = u0 - p0 - tx[rows, :]
                st = jnp.maximum(open_x, 0.0)
                dx = jnp.maximum(state[4, rows, :], (1.0 - jnp.exp(st * st * -4.0)) * w)
                state[4, rows, :] = dx
                sp = 1.0 - dx
                nx = sp * open_x
                ax = sp * (u1 - p1)
                open_y = u1 - pltpu.roll(u1, 1, 1) - ty[rows, :]
                st = jnp.maximum(open_y, 0.0)
                dy = jnp.maximum(state[5, rows, :], (1.0 - jnp.exp(st * st * -4.0)) * w)
                state[5, rows, :] = dy
                sp = 1.0 - dy
                ny = sp * open_y
                ay = sp * (u0 - pltpu.roll(u0, 1, 1))
                new = dict(
                    r0=r0, r1=r1, nx=nx, ax=ax, u0=u0, u1=u1,
                    sx=pltpu.roll(nx, 7, 0), sa=pltpu.roll(ax, 7, 0),
                    fy0=pltpu.roll(ay, fwide - 1, 1) - ay,
                    fy1=pltpu.roll(ny, fwide - 1, 1) - ny,
                )
            if old:
                rows = slice(8 * s - 8, 8 * s)
                nn = jnp.where(sub == 7, new["sx"], old["sx"])
                na = jnp.where(sub == 7, new["sa"], old["sa"])
                f0 = (nn - old["nx"]) + old["fy0"]
                f1 = (na - old["ax"]) + old["fy1"]
                v0, v1 = state[2, rows, :], state[3, rows, :]
                v0 = v0 + 0.4 * (f0 - 0.05 * v0)
                v1 = v1 + 0.4 * (f1 - 0.05 * v1)
                state[2, rows, :] = v0
                state[3, rows, :] = v1
                state[0, rows, :] = old["u0"] + 0.4 * v0
                state[1, rows, :] = old["u1"] + 0.4 * v1
            old = new
        return c

    lax.fori_loop(0, SUBSTEPS, substep, 0)

    dam_x = jnp.where(grow >= 1, state[4, own_r, 0:ww], 0.0)
    dam_y = jnp.where(gcol >= 1, state[5, own_r, 0:ww], 0.0)
    both = dam_x + dam_y
    for t in range(ww // 128):
        gap[t] = both[:, 128 * t : 128 * t + 128]
    rows2 = jnp.concatenate(
        [
            gap[t, pl.ds(0, ch, stride=2), :] + gap[t, pl.ds(1, ch, stride=2), :]
            for t in range(ww // 128)
        ],
        axis=1,
    )
    k_i, n_i = row_iota((256, 128)), lane_iota((256, 128))
    pos = (k_i % SEG).astype(F32)
    col = (2 * (n_i % 64)).astype(F32)
    tab = jnp.exp(jnp.abs(pos - col) * (-4.0 / SEG)) + jnp.exp(jnp.abs(pos - col - 1.0) * (-4.0 / SEG))
    tab = jnp.where(k_i // SEG == n_i // 64, tab * (1.0 / SEG), 0.0)
    npair = ww // 256
    glow = full_dot(
        jnp.concatenate([rows2[:, 256 * t : 256 * t + 256] for t in range(npair)], axis=0), tab
    )
    resist = jnp.concatenate([glow[ch * t : ch * t + ch] for t in range(npair)], axis=1)
    cond_own = (1.0 + 0.5 * tc[8 : 8 + ch, 0:cw]) / (1.0 + resist)
    cbuf[...] = cond_own
    second = neighbours(
        cbuf.at[:, 0:128], cbuf.at[:, cw - 128 : cw], cbuf.at[0:8], cbuf.at[ch - 8 : ch],
        ccl, ccr, crow.at[0], crow.at[1], ch, c_send, c_recv,
    )
    for copy in second:
        copy.start()

    dambuf[0] = dam_x.astype(jnp.bfloat16)
    dambuf[1] = dam_y.astype(jnp.bfloat16)
    puts = [
        pltpu.make_async_copy(src, dst, out_sem.at[i])
        for i, (src, dst) in enumerate(
            (
                (state.at[0:2, own_r, 0:ww], o_shift),
                (state.at[2:4, own_r, 0:ww], o_speed),
                (dambuf, o_dam),
                (warmbuf, o_warm),
            )
        )
    ]
    for copy in puts[0:3]:
        copy.start()

    pltpu.make_async_copy(arecv, arecv, a_sem.at[0]).wait()
    for k in range(nsl):
        ac[rpd * k : rpd * k + rpd, :] = arecv[k, 0]
        fc[rpd * k : rpd * k + rpd, :] = arecv[k, 1]

    for copy in second:
        copy.wait_recv()
    lane_k = lane_iota((crows, 128))
    cond = jnp.concatenate(
        [
            jnp.concatenate([crow[0], cbuf[...], crow[1]], axis=0),
            jnp.where(lane_k < 64, ccr[...], ccl[...]),
        ],
        axis=1,
    )
    crow_g = gx * ch - 8 + crow_i
    ccol_g = gy * cw + jnp.where(clane_i < cw + 64, clane_i, clane_i - wide)

    def four(x):
        return (
            pltpu.roll(x, 1, 0),
            pltpu.roll(x, crows - 1, 0),
            pltpu.roll(x, 1, 1),
            pltpu.roll(x, wide - 1, 1),
        )

    masks = (
        crow_g >= 1,
        crow_g <= ch * n_gx - 2,
        ccol_g >= 1,
        ccol_g <= cw * n_gy - 2,
    )
    faces = [
        jnp.where(m, 0.5 * (cond + nb), 0.0) for m, nb in zip(masks, four(cond))
    ]
    offsum = faces[0] + faces[1] + faces[2] + faces[3]
    diagonal = ac[...] + offsum
    ratio = offsum / diagonal
    peak = jnp.max(ratio[8 : 8 + ch, 0:cw])
    msend[...] = jnp.full((8, 128), peak, F32)

    def tell(k, c):
        t = lax.rem(me + k, ndev)
        remote(
            msend, mrecv.at[k - 1], m_sem.at[1], m_sem.at[0], (t // n_gy, t % n_gy)
        ).start()
        return c

    lax.fori_loop(1, ndev, tell, 0)

    t_all = tc[...]
    near = sum(f * nb for f, nb in zip(faces, four(t_all)))
    z = (fc[...] - (diagonal * t_all - near)) / diagonal
    faces = [f / diagonal for f in faces]
    for j in range(4):
        if j:
            z = z - sum(f * nb for f, nb in zip(faces, four(z)))
        for k in range(n_gy):
            zsend[k, j] = z[8 + rpd * k : 8 + rpd * k + rpd, 0:cw]

    def home(k, c):
        t = lax.rem(gy + k, n_gy)
        remote(zsend.at[t], zrecv.at[gy], z_sem.at[1], z_sem.at[0], (gx, t)).start()
        return c

    lax.fori_loop(1, n_gy, home, 0)
    pltpu.make_async_copy(zsend.at[gy], zrecv.at[gy], z_sem.at[0]).start()

    pltpu.make_async_copy(mrecv, mrecv, m_sem.at[0]).wait()
    peak = jnp.maximum(jnp.max(mrecv[...], axis=0), msend[...])[0:1, :]
    low, high = 1.0 - peak, 1.0 + peak
    center = 0.5 * (high + low)
    spread = 0.5 * (high - low)
    sigma = center / spread
    rho = 1.0 / sigma
    zero = jnp.zeros_like(center)
    e = [zero + 1.0, zero, zero, zero]
    d = [1.0 / center, zero, zero, zero]
    total = list(d)
    for _ in range(3):
        e = [e[0]] + [e[i] - d[i - 1] for i in range(1, 4)]
        rho_next = 1.0 / (2.0 * sigma - rho)
        d = [rho_next * rho * d[i] + (2.0 * rho_next / spread) * e[i] for i in range(4)]
        total = [a + b for a, b in zip(total, d)]
        rho = rho_next
    total = [jnp.concatenate([c] * (cw // 128), axis=1) for c in total]

    pltpu.make_async_copy(zrecv, zrecv, z_sem.at[0]).wait()
    for k in range(n_gy):
        x = warm[:, cw * k : cw * k + cw]
        for j in range(4):
            x = x + total[j] * zrecv[k, j]
        warmbuf[:, cw * k : cw * k + cw] = x
    puts[3].start()

    for copy in second:
        copy.wait_send()
    spread_sent(tsend, trecv, t_sem)
    spread_sent(asend, arecv, a_sem)
    part = pl.ds(0, n_gy - 1)
    remote(zsend.at[part], zrecv.at[part], z_sem.at[1], z_sem.at[0], (gx, right)).wait_send()
    remote(mrecv, mrecv, m_sem.at[1], m_sem.at[0], (gx, right)).wait_send()
    for copy in puts:
        copy.wait()


def put_out(*refs):
    src, dst, via, (isem, osem) = refs[0:4], refs[4:8], refs[8:12], refs[12:14]
    into = [pltpu.make_async_copy(src[i], via[i], isem.at[i]) for i in range(4)]
    out = [pltpu.make_async_copy(via[i], dst[i], osem.at[i]) for i in range(4)]
    for copy in into:
        copy.start()
    for i in range(4):
        into[i].wait()
        out[i].start()
    for copy in out:
        copy.wait()


def per_device(n_gx, n_gy, shift, speed, level, mark, warm, store, film, bath):
    _, hh, ww = shift.shape
    rpd, _ = warm.shape
    cw, ch = ww // 2, hh // 2
    wide, fwide = cw + 128, ww + 128
    crows, frows = ch + 16, hh + 2 * HALO
    nsl = n_gy + 2 * (HALO // rpd)
    vm = lambda *s: pltpu.VMEM(s, F32)
    dma = lambda n: pltpu.SemaphoreType.DMA((n,))
    hbm = pl.BlockSpec(memory_space=pltpu.HBM)
    outs = pl.pallas_call(
        functools.partial(kernel, n_gx, n_gy),
        out_shape=(
            jax.ShapeDtypeStruct(shift.shape, F32),
            jax.ShapeDtypeStruct(speed.shape, F32),
            jax.ShapeDtypeStruct(level.shape, jnp.bfloat16),
            jax.ShapeDtypeStruct(warm.shape, F32),
        ),
        in_specs=[hbm] * 3 + [pl.BlockSpec(memory_space=pltpu.SMEM)] + [hbm] * 4,
        out_specs=(hbm,) * 4,
        scratch_shapes=[
            vm(n_gy, rpd, wide),
            vm(nsl, rpd, wide),
            vm(n_gy, 2, rpd, wide),
            vm(nsl, 2, rpd, wide),
            vm(hh, 128),
            vm(hh, 128),
            vm(frows, 128),
            vm(frows, 128),
            vm(2, 8, 128),
            vm(2, 8, 128),
            pltpu.VMEM(level.shape, level.dtype),
            vm(*warm.shape),
            vm(*warm.shape),
            vm(*warm.shape),
            vm(*warm.shape),
            vm(6, frows, fwide),
            vm(frows, fwide),
            vm(frows, fwide),
            vm(frows, fwide),
            vm(crows, wide),
            vm(crows, wide),
            vm(crows, wide),
            vm(wide // 128, frows, 128),
            vm(ww // 128, hh, 128),
            vm(ch, cw),
            vm(2, 8, cw),
            vm(crows, 128),
            vm(crows, 128),
            vm(n_gy, 4, rpd, cw),
            vm(n_gy, 4, rpd, cw),
            vm(8, 128),
            vm(n_gx * n_gy - 1, 8, 128),
            dma(10),
            dma(10),
            dma(4),
            dma(4),
            dma(8),
            dma(8),
            dma(2),
            dma(2),
            dma(7),
            pltpu.VMEM(level.shape, jnp.bfloat16),
            vm(*warm.shape),
            dma(4),
        ],
        compiler_params=pltpu.CompilerParams(
            collective_id=0, has_side_effects=True
        ),
    )(shift, speed, level, mark.reshape(1, hh // SR), warm, store, film, bath)
    return pl.pallas_call(
        put_out,
        out_shape=tuple(jax.ShapeDtypeStruct(o.shape, o.dtype) for o in outs),
        in_specs=[hbm] * 4,
        out_specs=(hbm,) * 4,
        scratch_shapes=[pltpu.VMEM(o.shape, o.dtype) for o in outs] + [dma(4), dma(4)],
    )(*outs)


def solution(mesh):
    rows = P(("gx", "gy"), None)
    plate = P(None, "gx", "gy")
    return jax.shard_map(
        functools.partial(per_device, mesh.shape["gx"], mesh.shape["gy"]),
        mesh=mesh,
        in_specs=(plate, plate, plate, P("gx", "gy"), rows, rows, rows, rows),
        out_specs=(plate, plate, plate, rows),
        check_vma=False,
    )
```

```python
import functools

import jax
import jax.numpy as jnp
from jax import lax
from jax.experimental import pallas as pl
from jax.experimental.pallas import tpu as pltpu
from jax.sharding import PartitionSpec as P

SR = 8
SEG = 128
SUBSTEPS = 8
HALO = 8
MESH = pl.DeviceIdType.MESH
F32 = jnp.float32


def lane_iota(shape):
    return lax.broadcasted_iota(jnp.int32, shape, 1)


def row_iota(shape):
    return lax.broadcasted_iota(jnp.int32, shape, 0)


def full_dot(a, b):
    return jnp.dot(a, b, precision=lax.Precision.HIGHEST, preferred_element_type=F32)


def kernel(
    n_gx,
    n_gy,
    shift,
    speed,
    level_h,
    mark,
    warm_h,
    store_h,
    film_h,
    bath_h,
    o_shift,
    o_speed,
    o_dam,
    o_warm,
    tsend,
    trecv,
    asend,
    arecv,
    pk_l,
    pk_r,
    rk_l,
    rk_r,
    wsend,
    wrecv,
    rowsend,
    rowrecv,
    keep,
    hist,
    level,
    warm,
    store,
    film,
    bath,
    state,
    wt,
    tx,
    ty,
    tc,
    ac,
    fc,
    widebuf,
    gap,
    cbuf,
    crow,
    ccl,
    ccr,
    zsend,
    zrecv,
    msend,
    mrecv,
    nb_send,
    nb_recv,
    t_sem,
    a_sem,
    c_send,
    c_recv,
    z_sem,
    m_sem,
    in_sem,
    dambuf,
    warmbuf,
    out_sem,
):
    ndev = n_gx * n_gy
    gx = lax.axis_index("gx")
    gy = lax.axis_index("gy")
    me = gx * n_gy + gy
    _, hh, ww = shift.shape
    rpd, _ = warm_h.shape
    cw = ww // 2
    ch = hh // 2
    hb = HALO // rpd
    nsl = n_gy + 2 * hb
    up = lax.rem(gx + n_gx - 1, n_gx)
    down = lax.rem(gx + 1, n_gx)
    left = lax.rem(gy + n_gy - 1, n_gy)
    right = lax.rem(gy + 1, n_gy)

    own_r = slice(HALO, HALO + hh)
    loads = [
        pltpu.make_async_copy(src, dst, in_sem.at[i])
        for i, (src, dst) in enumerate(
            (
                (warm_h, warm),
                (level_h, level),
                (shift, state.at[0:2, own_r, 0:ww]),
                (speed, state.at[2:4, own_r, 0:ww]),
                (store_h, store),
                (film_h, film),
                (bath_h, bath),
            )
        )
    ]
    for copy in loads:
        copy.start()
    barrier = pltpu.get_barrier_semaphore()

    def greet(k, c):
        t = lax.rem(me + k, ndev)
        pl.semaphore_signal(barrier, inc=1, device_id=(t // n_gy, t % n_gy), device_id_type=MESH)
        return c

    lax.fori_loop(1, ndev, greet, 0)

    lane = lane_iota((hh, 128))
    for s in range(hh // SR):
        wt[HALO + SR * s : HALO + SR * s + SR, 0:ww] = jnp.full((SR, ww), mark[0, s], jnp.int32).astype(F32)
    w_own = wt[own_r, 0:ww]
    grow = gx * hh + row_iota((hh, ww))
    gcol = gy * ww + lane_iota((hh, ww))
    loads[1].wait()
    state[4, own_r, 0:ww] = jnp.where(grow >= 1, level[0].astype(F32) * 0.125 * w_own, 1.0)
    state[5, own_r, 0:ww] = jnp.where(gcol >= 1, level[1].astype(F32) * 0.125 * w_own, 1.0)
    wsend[0] = wt[HALO : HALO + 8, 0:128]
    wsend[1] = wt[HALO + hh - 8 : HALO + hh, 0:128]
    loads[2].wait()
    loads[3].wait()
    acc_l = jnp.zeros((hh, 128), F32)
    acc_r = jnp.zeros((hh, 128), F32)
    for f in range(7):
        field = state.at[f] if f < 6 else wt
        first, last = field[own_r, 0:128], field[own_r, ww - 128 : ww]
        here = (lane >= 8 * f) & (lane < 8 * f + 8)
        first = pltpu.roll(first, 8 * f, 1) if f else first
        acc_l = jnp.where(here, first, acc_l)
        acc_r = jnp.where(here, pltpu.roll(last, 8 * f + 8, 1), acc_r)
        if f < 6:
            rowsend[0, f] = field[HALO : HALO + 8, 0:ww]
            rowsend[1, f] = field[HALO + hh - 8 : HALO + hh, 0:ww]
    pk_l[...] = acc_l
    pk_r[...] = acc_r

    lane_c = lane_iota((rpd, 128))

    def chunk(value, k):
        after = value[:, (cw * (k + 1)) % (cw * n_gy) :][:, 0:128]
        before = value[:, (cw * k - 128) % (cw * n_gy) :][:, 0:128]
        return value[:, cw * k : cw * k + cw], jnp.where(lane_c < 64, after, before)

    for i in (0, 4, 5, 6):
        loads[i].wait()
    t_own = warm[...]
    base = store[...] + film[...]
    force_own = store[...] * t_own + film[...] * bath[...]
    for k in range(n_gy):
        main, edge = chunk(t_own, k)
        tsend[k, :, 0:cw] = main
        tsend[k, :, cw : cw + 128] = edge
        for q, val in enumerate((base, force_own)):
            main, edge = chunk(val, k)
            asend[k, q, :, 0:cw] = main
            asend[k, q, :, cw : cw + 128] = edge

    pl.semaphore_wait(barrier, ndev - 1)

    def remote(src, dst, ssem, rsem, where):
        return pltpu.make_async_remote_copy(
            src_ref=src, dst_ref=dst, send_sem=ssem, recv_sem=rsem, device_id=where,
            device_id_type=MESH,
        )

    def neighbours(send_l, send_r, row_u, row_d, recv_l, recv_r, got_u, got_d, rows, ssem, rsem):
        top, end = slice(0, 8), slice(rows - 8, rows)
        lo, mid, hi = slice(0, 8), slice(8, rows + 8), slice(rows + 8, rows + 16)
        return [
            remote(row_u, got_d, ssem.at[0], rsem.at[0], (up, gy)),
            remote(row_d, got_u, ssem.at[1], rsem.at[1], (down, gy)),
            remote(send_l, recv_r.at[mid], ssem.at[2], rsem.at[2], (gx, left)),
            remote(send_r, recv_l.at[mid], ssem.at[3], rsem.at[3], (gx, right)),
            remote(send_l.at[top], recv_r.at[hi], ssem.at[4], rsem.at[4], (up, left)),
            remote(send_r.at[top], recv_l.at[hi], ssem.at[5], rsem.at[5], (up, right)),
            remote(send_l.at[end], recv_r.at[lo], ssem.at[6], rsem.at[6], (down, left)),
            remote(send_r.at[end], recv_l.at[lo], ssem.at[7], rsem.at[7], (down, right)),
        ]

    first = neighbours(
        pk_l,
        pk_r,
        rowsend.at[0],
        rowsend.at[1],
        rk_l,
        rk_r,
        rowrecv.at[0],
        rowrecv.at[1],
        hh,
        nb_send,
        nb_recv,
    ) + [
        remote(wsend.at[0], wrecv.at[1], nb_send.at[8], nb_recv.at[8], (up, gy)),
        remote(wsend.at[1], wrecv.at[0], nb_send.at[9], nb_recv.at[9], (down, gy)),
    ]

    def spread_out(send, recv, sem):
        def along(k, c):
            t = lax.rem(gy + k, n_gy)
            remote(send.at[t], recv.at[gy + hb], sem.at[1], sem.at[0], (gx, t)).start()
            return c

        lax.fori_loop(1, n_gy, along, 0)
        pltpu.make_async_copy(send.at[gy], recv.at[gy + hb], sem.at[0]).start()

        @pl.when(gy < hb)
        def _():
            def go(k, c):
                remote(
                    send.at[k], recv.at[gy + hb + n_gy], sem.at[2], sem.at[0], (up, k)
                ).start()
                return c

            lax.fori_loop(0, n_gy, go, 0)

        @pl.when(gy >= n_gy - hb)
        def _():
            def go(k, c):
                remote(
                    send.at[k], recv.at[gy - (n_gy - hb)], sem.at[3], sem.at[0], (down, k)
                ).start()
                return c

            lax.fori_loop(0, n_gy, go, 0)

    def spread_sent(send, recv, sem):
        part = pl.ds(0, n_gy - 1)
        remote(send.at[part], recv.at[part], sem.at[1], sem.at[0], (gx, right)).wait_send()
        whole = pl.ds(0, n_gy)

        @pl.when(gy < hb)
        def _():
            remote(send, recv.at[whole], sem.at[2], sem.at[0], (up, gy)).wait_send()

        @pl.when(gy >= n_gy - hb)
        def _():
            remote(send, recv.at[whole], sem.at[3], sem.at[0], (down, gy)).wait_send()

    spread_out(tsend, trecv, t_sem)
    for copy in first:
        copy.start()

    pltpu.make_async_copy(trecv, trecv, t_sem.at[0]).wait()
    spread_out(asend, arecv, a_sem)
    crows = ch + 16
    for k in range(nsl):
        tc[rpd * k : rpd * k + rpd, :] = trecv[k]
    cshape = (crows, cw + 128)
    crow_i, clane_i = row_iota(cshape), lane_iota(cshape)
    t_all = tc[...]
    p = t_all
    p = jnp.where((gx == 0) & (crow_i < 8), t_all[8:9, :], p)
    p = jnp.where((gx == n_gx - 1) & (crow_i >= ch + 8), t_all[ch + 7 : ch + 8, :], p)
    wide = cw + 128
    q = jnp.where((gy == 0) & (clane_i == wide - 1), pltpu.roll(p, wide - 1, 1), p)
    q = jnp.where((gy == n_gy - 1) & (clane_i == cw), pltpu.roll(p, 1, 1), q)
    even = 0.75 * q + 0.25 * pltpu.roll(q, 1, 0)
    odd = 0.75 * q + 0.25 * pltpu.roll(q, crows - 1, 0)
    frows = hh + 2 * HALO
    need = frows // 2
    ntile = wide // 128
    for t in range(ntile):
        cols = slice(128 * t, 128 * t + 128)
        widebuf[t, pl.ds(0, need, stride=2), :] = even[4 : 4 + need, cols]
        widebuf[t, pl.ds(1, need, stride=2), :] = odd[4 : 4 + need, cols]
    r = jnp.concatenate([widebuf[t] for t in range(ntile)], axis=1)
    ecol = 0.75 * r + 0.25 * pltpu.roll(r, 1, 1)
    ocol = 0.75 * r + 0.25 * pltpu.roll(r, wide - 1, 1)
    k_i, n_i = row_iota((256, 256)), lane_iota((256, 256))
    weave = (n_i == jnp.where(k_i < 128, 2 * k_i, 2 * k_i - 255)).astype(F32)
    stack = jnp.concatenate(
        [
            jnp.concatenate([ecol[:, 128 * t : 128 * t + 128], ocol[:, 128 * t : 128 * t + 128]], 1)
            for t in range(ntile)
        ],
        axis=0,
    )
    woven = full_dot(stack, weave)
    lane_f = lane_iota((frows, 128))
    pieces = [woven[frows * t : frows * t + frows] for t in range(ntile)]
    edge = jnp.where(lane_f < 64, pieces[-1][:, 0:128], pieces[-1][:, 128:256])
    fine = jnp.concatenate(pieces[:-1] + [edge], axis=1)
    fwide = ww + 128
    tx[...] = 0.6 * (0.5 * (fine + pltpu.roll(fine, 1, 0)))
    ty[...] = 0.6 * (0.5 * (fine + pltpu.roll(fine, 1, 1)))

    for copy in first[2:8]:
        copy.wait_recv()
    got_l, got_r = rk_l[...], rk_r[...]
    for f in range(7):
        from_r = pltpu.roll(got_r, 128 - 8 * f, 1) if f else got_r
        from_l = pltpu.roll(got_l, 120 - 8 * f, 1)
        side = jnp.where(lane_f < 8, from_r, jnp.where(lane_f >= 120, from_l, 0.0))
        if f == 5:
            off_l = (gy == 0) & (lane_f >= 64)
            off_r = (gy == n_gy - 1) & (lane_f < 64)
            side = jnp.where(off_l | off_r, 1.0, side)
        target = state.at[f] if f < 6 else wt
        target[:, ww:fwide] = side
    sub = row_iota((8, fwide))
    last_strip = frows // 8 - 1

    def edges(s, old):
        rows = slice(8 * s, 8 * s + 8)
        u0, u1 = state[0, rows, :], state[1, rows, :]
        w = wt[rows, :]
        r0, r1 = pltpu.roll(u0, 1, 0), pltpu.roll(u1, 1, 0)
        p0 = jnp.where(sub == 0, old["r0"], r0) if old else r0
        p1 = jnp.where(sub == 0, old["r1"], r1) if old else r1
        open_x = u0 - p0 - tx[rows, :]
        st = jnp.maximum(open_x, 0.0)
        dx = jnp.maximum(state[4, rows, :], (1.0 - jnp.exp(st * st * -4.0)) * w)
        state[4, rows, :] = dx
        sp = 1.0 - dx
        nx = sp * open_x
        ax = sp * (u1 - p1)
        open_y = u1 - pltpu.roll(u1, 1, 1) - ty[rows, :]
        st = jnp.maximum(open_y, 0.0)
        dy = jnp.maximum(state[5, rows, :], (1.0 - jnp.exp(st * st * -4.0)) * w)
        state[5, rows, :] = dy
        sp = 1.0 - dy
        ny = sp * open_y
        ay = sp * (u0 - pltpu.roll(u0, 1, 1))
        return dict(
            r0=r0, r1=r1, nx=nx, ax=ax, u0=u0, u1=u1,
            sx=pltpu.roll(nx, 7, 0), sa=pltpu.roll(ax, 7, 0),
            fy0=pltpu.roll(ay, fwide - 1, 1) - ay,
            fy1=pltpu.roll(ny, fwide - 1, 1) - ny,
        )

    def advance(s, old, new):
        rows = slice(8 * s, 8 * s + 8)
        nn = jnp.where(sub == 7, new["sx"], old["sx"])
        na = jnp.where(sub == 7, new["sa"], old["sa"])
        f0 = (nn - old["nx"]) + old["fy0"]
        f1 = (na - old["ax"]) + old["fy1"]
        v0, v1 = state[2, rows, :], state[3, rows, :]
        v0 = v0 + 0.4 * (f0 - 0.05 * v0)
        v1 = v1 + 0.4 * (f1 - 0.05 * v1)
        state[2, rows, :] = v0
        state[3, rows, :] = v1
        state[0, rows, :] = old["u0"] + 0.4 * v0
        state[1, rows, :] = old["u1"] + 0.4 * v1

    redo = (slice(8, 16), slice(8 * last_strip - 8, 8 * last_strip))
    for i, rows in enumerate(redo):
        keep[i] = state[:, rows, :]

    def interior(t, c):
        old = None
        for s in range(1, last_strip):
            new = edges(s, old)
            if s == 2:
                hist[t, 0] = new["sx"]
                hist[t, 1] = new["sa"]
            if s == last_strip - 2:
                hist[t, 2] = new["r0"]
                hist[t, 3] = new["r1"]
            if old:
                advance(s - 1, old, new)
            old = new
        advance(last_strip - 1, old, old)
        return c

    lax.fori_loop(0, SUBSTEPS, interior, 0)

    for copy in first[0:2] + first[8:10]:
        copy.wait_recv()
    for i, rows in enumerate(redo):
        state[:, rows, :] = keep[i]
    for side_row, at in ((0, 0), (1, hh + HALO)):
        state[:, at : at + 8, 0:ww] = rowrecv[side_row]
        for t in range(ww // 128):
            wt[at : at + 8, 128 * t : 128 * t + 128] = wrecv[side_row]

    @pl.when(gx == 0)
    def _():
        state[4, 0:8, :] = jnp.ones((8, fwide), F32)

    @pl.when(gx == n_gx - 1)
    def _():
        state[4, hh + HALO : hh + HALO + 8, :] = jnp.ones((8, fwide), F32)

    def border(t, c):
        e0 = edges(0, None)
        e1 = edges(1, e0)
        advance(0, e0, e1)
        advance(1, e1, dict(sx=hist[t, 0], sa=hist[t, 1]))
        e8 = edges(last_strip - 1, dict(r0=hist[t, 2], r1=hist[t, 3]))
        e9 = edges(last_strip, e8)
        advance(last_strip - 1, e8, e9)
        advance(last_strip, e9, e9)
        return c

    lax.fori_loop(0, SUBSTEPS, border, 0)

    dam_x = jnp.where(grow >= 1, state[4, own_r, 0:ww], 0.0)
    dam_y = jnp.where(gcol >= 1, state[5, own_r, 0:ww], 0.0)
    both = dam_x + dam_y
    for t in range(ww // 128):
        gap[t] = both[:, 128 * t : 128 * t + 128]
    rows2 = jnp.concatenate(
        [
            gap[t, pl.ds(0, ch, stride=2), :] + gap[t, pl.ds(1, ch, stride=2), :]
            for t in range(ww // 128)
        ],
        axis=1,
    )
    k_i, n_i = row_iota((256, 128)), lane_iota((256, 128))
    pos = (k_i % SEG).astype(F32)
    col = (2 * (n_i % 64)).astype(F32)
    tab = jnp.exp(jnp.abs(pos - col) * (-4.0 / SEG)) + jnp.exp(jnp.abs(pos - col - 1.0) * (-4.0 / SEG))
    tab = jnp.where(k_i // SEG == n_i // 64, tab * (1.0 / SEG), 0.0)
    npair = ww // 256
    glow = full_dot(
        jnp.concatenate([rows2[:, 256 * t : 256 * t + 256] for t in range(npair)], axis=0), tab
    )
    resist = jnp.concatenate([glow[ch * t : ch * t + ch] for t in range(npair)], axis=1)
    cond_own = (1.0 + 0.5 * tc[8 : 8 + ch, 0:cw]) / (1.0 + resist)
    cbuf[...] = cond_own
    second = neighbours(
        cbuf.at[:, 0:128], cbuf.at[:, cw - 128 : cw], cbuf.at[0:8], cbuf.at[ch - 8 : ch],
        ccl, ccr, crow.at[0], crow.at[1], ch, c_send, c_recv,
    )
    for copy in second:
        copy.start()

    dambuf[0] = dam_x.astype(jnp.bfloat16)
    dambuf[1] = dam_y.astype(jnp.bfloat16)
    puts = [
        pltpu.make_async_copy(src, dst, out_sem.at[i])
        for i, (src, dst) in enumerate(
            (
                (state.at[0:2, own_r, 0:ww], o_shift),
                (state.at[2:4, own_r, 0:ww], o_speed),
                (dambuf, o_dam),
                (warmbuf, o_warm),
            )
        )
    ]
    for copy in puts[0:3]:
        copy.start()

    pltpu.make_async_copy(arecv, arecv, a_sem.at[0]).wait()
    for k in range(nsl):
        ac[rpd * k : rpd * k + rpd, :] = arecv[k, 0]
        fc[rpd * k : rpd * k + rpd, :] = arecv[k, 1]

    for copy in second:
        copy.wait_recv()
    lane_k = lane_iota((crows, 128))
    cond = jnp.concatenate(
        [
            jnp.concatenate([crow[0], cbuf[...], crow[1]], axis=0),
            jnp.where(lane_k < 64, ccr[...], ccl[...]),
        ],
        axis=1,
    )
    crow_g = gx * ch - 8 + crow_i
    ccol_g = gy * cw + jnp.where(clane_i < cw + 64, clane_i, clane_i - wide)

    def four(x):
        return (
            pltpu.roll(x, 1, 0),
            pltpu.roll(x, crows - 1, 0),
            pltpu.roll(x, 1, 1),
            pltpu.roll(x, wide - 1, 1),
        )

    masks = (
        crow_g >= 1,
        crow_g <= ch * n_gx - 2,
        ccol_g >= 1,
        ccol_g <= cw * n_gy - 2,
    )
    faces = [
        jnp.where(m, 0.5 * (cond + nb), 0.0) for m, nb in zip(masks, four(cond))
    ]
    offsum = faces[0] + faces[1] + faces[2] + faces[3]
    diagonal = ac[...] + offsum
    ratio = offsum / diagonal
    peak = jnp.max(ratio[8 : 8 + ch, 0:cw])
    msend[...] = jnp.full((8, 128), peak, F32)

    def tell(k, c):
        t = lax.rem(me + k, ndev)
        remote(
            msend, mrecv.at[k - 1], m_sem.at[1], m_sem.at[0], (t // n_gy, t % n_gy)
        ).start()
        return c

    lax.fori_loop(1, ndev, tell, 0)

    t_all = tc[...]
    near = sum(f * nb for f, nb in zip(faces, four(t_all)))
    z = (fc[...] - (diagonal * t_all - near)) / diagonal
    faces = [f / diagonal for f in faces]
    for j in range(4):
        if j:
            z = z - sum(f * nb for f, nb in zip(faces, four(z)))
        for k in range(n_gy):
            zsend[k, j] = z[8 + rpd * k : 8 + rpd * k + rpd, 0:cw]

    def home(k, c):
        t = lax.rem(gy + k, n_gy)
        remote(zsend.at[t], zrecv.at[gy], z_sem.at[1], z_sem.at[0], (gx, t)).start()
        return c

    lax.fori_loop(1, n_gy, home, 0)
    pltpu.make_async_copy(zsend.at[gy], zrecv.at[gy], z_sem.at[0]).start()

    pltpu.make_async_copy(mrecv, mrecv, m_sem.at[0]).wait()
    peak = jnp.maximum(jnp.max(mrecv[...], axis=0), msend[...])[0:1, :]
    low, high = 1.0 - peak, 1.0 + peak
    center = 0.5 * (high + low)
    spread = 0.5 * (high - low)
    sigma = center / spread
    rho = 1.0 / sigma
    zero = jnp.zeros_like(center)
    e = [zero + 1.0, zero, zero, zero]
    d = [1.0 / center, zero, zero, zero]
    total = list(d)
    for _ in range(3):
        e = [e[0]] + [e[i] - d[i - 1] for i in range(1, 4)]
        rho_next = 1.0 / (2.0 * sigma - rho)
        d = [rho_next * rho * d[i] + (2.0 * rho_next / spread) * e[i] for i in range(4)]
        total = [a + b for a, b in zip(total, d)]
        rho = rho_next
    total = [jnp.concatenate([c] * (cw // 128), axis=1) for c in total]

    pltpu.make_async_copy(zrecv, zrecv, z_sem.at[0]).wait()
    for k in range(n_gy):
        x = warm[:, cw * k : cw * k + cw]
        for j in range(4):
            x = x + total[j] * zrecv[k, j]
        warmbuf[:, cw * k : cw * k + cw] = x
    puts[3].start()

    for copy in first + second:
        copy.wait_send()
    spread_sent(tsend, trecv, t_sem)
    spread_sent(asend, arecv, a_sem)
    part = pl.ds(0, n_gy - 1)
    remote(zsend.at[part], zrecv.at[part], z_sem.at[1], z_sem.at[0], (gx, right)).wait_send()
    remote(mrecv, mrecv, m_sem.at[1], m_sem.at[0], (gx, right)).wait_send()
    for copy in puts:
        copy.wait()


def put_out(*refs):
    src, dst, via, (isem, osem) = refs[0:4], refs[4:8], refs[8:12], refs[12:14]
    into = [pltpu.make_async_copy(src[i], via[i], isem.at[i]) for i in range(4)]
    out = [pltpu.make_async_copy(via[i], dst[i], osem.at[i]) for i in range(4)]
    for copy in into:
        copy.start()
    for i in range(4):
        into[i].wait()
        out[i].start()
    for copy in out:
        copy.wait()


def per_device(n_gx, n_gy, shift, speed, level, mark, warm, store, film, bath):
    _, hh, ww = shift.shape
    rpd, _ = warm.shape
    cw, ch = ww // 2, hh // 2
    wide, fwide = cw + 128, ww + 128
    crows, frows = ch + 16, hh + 2 * HALO
    nsl = n_gy + 2 * (HALO // rpd)
    vm = lambda *s: pltpu.VMEM(s, F32)
    dma = lambda n: pltpu.SemaphoreType.DMA((n,))
    hbm = pl.BlockSpec(memory_space=pltpu.HBM)
    outs = pl.pallas_call(
        functools.partial(kernel, n_gx, n_gy),
        out_shape=(
            jax.ShapeDtypeStruct(shift.shape, F32),
            jax.ShapeDtypeStruct(speed.shape, F32),
            jax.ShapeDtypeStruct(level.shape, jnp.bfloat16),
            jax.ShapeDtypeStruct(warm.shape, F32),
        ),
        in_specs=[hbm] * 3 + [pl.BlockSpec(memory_space=pltpu.SMEM)] + [hbm] * 4,
        out_specs=(hbm,) * 4,
        scratch_shapes=[
            vm(n_gy, rpd, wide),
            vm(nsl, rpd, wide),
            vm(n_gy, 2, rpd, wide),
            vm(nsl, 2, rpd, wide),
            vm(hh, 128),
            vm(hh, 128),
            vm(frows, 128),
            vm(frows, 128),
            vm(2, 8, 128),
            vm(2, 8, 128),
            vm(2, 6, 8, ww),
            vm(2, 6, 8, ww),
            vm(2, 6, 8, fwide),
            vm(SUBSTEPS, 4, 8, fwide),
            pltpu.VMEM(level.shape, level.dtype),
            vm(*warm.shape),
            vm(*warm.shape),
            vm(*warm.shape),
            vm(*warm.shape),
            vm(6, frows, fwide),
            vm(frows, fwide),
            vm(frows, fwide),
            vm(frows, fwide),
            vm(crows, wide),
            vm(crows, wide),
            vm(crows, wide),
            vm(wide // 128, frows, 128),
            vm(ww // 128, hh, 128),
            vm(ch, cw),
            vm(2, 8, cw),
            vm(crows, 128),
            vm(crows, 128),
            vm(n_gy, 4, rpd, cw),
            vm(n_gy, 4, rpd, cw),
            vm(8, 128),
            vm(n_gx * n_gy - 1, 8, 128),
            dma(10),
            dma(10),
            dma(4),
            dma(4),
            dma(8),
            dma(8),
            dma(2),
            dma(2),
            dma(7),
            pltpu.VMEM(level.shape, jnp.bfloat16),
            vm(*warm.shape),
            dma(4),
        ],
        compiler_params=pltpu.CompilerParams(
            collective_id=0, has_side_effects=True
        ),
    )(shift, speed, level, mark.reshape(1, hh // SR), warm, store, film, bath)
    return pl.pallas_call(
        put_out,
        out_shape=tuple(jax.ShapeDtypeStruct(o.shape, o.dtype) for o in outs),
        in_specs=[hbm] * 4,
        out_specs=(hbm,) * 4,
        scratch_shapes=[pltpu.VMEM(o.shape, o.dtype) for o in outs] + [dma(4), dma(4)],
    )(*outs)


def solution(mesh):
    rows = P(("gx", "gy"), None)
    plate = P(None, "gx", "gy")
    return jax.shard_map(
        functools.partial(per_device, mesh.shape["gx"], mesh.shape["gy"]),
        mesh=mesh,
        in_specs=(plate, plate, plate, P("gx", "gy"), rows, rows, rows, rows),
        out_specs=(plate, plate, plate, rows),
        check_vma=False,
    )
```

```python
import functools

import jax
import jax.numpy as jnp
from jax import lax
from jax.experimental import pallas as pl
from jax.experimental.pallas import tpu as pltpu
from jax.sharding import PartitionSpec as P

SR = 8
SEG = 128
SUBSTEPS = 8
HALO = 8
MESH = pl.DeviceIdType.MESH
F32 = jnp.float32


def lane_iota(shape):
    return lax.broadcasted_iota(jnp.int32, shape, 1)


def row_iota(shape):
    return lax.broadcasted_iota(jnp.int32, shape, 0)


def full_dot(a, b):
    return jnp.dot(a, b, precision=lax.Precision.HIGHEST, preferred_element_type=F32)


def kernel(
    n_gx,
    n_gy,
    shift,
    speed,
    level_h,
    mark,
    warm_h,
    store_h,
    film_h,
    bath_h,
    o_shift,
    o_speed,
    o_dam,
    o_warm,
    tsend,
    trecv,
    asend,
    arecv,
    pk_l,
    pk_r,
    rk_l,
    rk_r,
    wsend,
    wrecv,
    rowsend,
    rowrecv,
    keep,
    hist,
    level,
    warm,
    store,
    film,
    bath,
    state,
    wt,
    tx,
    ty,
    tc,
    acf,
    widebuf,
    gap,
    cbuf,
    crow,
    ccl,
    ccr,
    zsend,
    zrecv,
    msend,
    mrecv,
    nb_send,
    nb_recv,
    t_sem,
    a_sem,
    c_send,
    c_recv,
    z_sem,
    m_sem,
    in_sem,
    dambuf,
    warmbuf,
    out_sem,
):
    ndev = n_gx * n_gy
    gx = lax.axis_index("gx")
    gy = lax.axis_index("gy")
    me = gx * n_gy + gy
    _, hh, ww = shift.shape
    rpd, _ = warm_h.shape
    cw = ww // 2
    ch = hh // 2
    hb = HALO // rpd
    nsl = n_gy + 2 * hb
    up = lax.rem(gx + n_gx - 1, n_gx)
    down = lax.rem(gx + 1, n_gx)
    left = lax.rem(gy + n_gy - 1, n_gy)
    right = lax.rem(gy + 1, n_gy)

    own_r = slice(HALO, HALO + hh)
    loads = [
        pltpu.make_async_copy(src, dst, in_sem.at[i])
        for i, (src, dst) in enumerate(
            (
                (warm_h, warm),
                (level_h, level),
                (shift, state.at[0:2, own_r, 0:ww]),
                (speed, state.at[2:4, own_r, 0:ww]),
                (store_h, store),
                (film_h, film),
                (bath_h, bath),
            )
        )
    ]
    for copy in loads:
        copy.start()
    barrier = pltpu.get_barrier_semaphore()

    def greet(k, c):
        t = lax.rem(me + k, ndev)
        pl.semaphore_signal(barrier, inc=1, device_id=(t // n_gy, t % n_gy), device_id_type=MESH)
        return c

    lax.fori_loop(1, ndev, greet, 0)

    lane = lane_iota((hh, 128))
    for s in range(hh // SR):
        wt[HALO + SR * s : HALO + SR * s + SR, 0:ww] = jnp.full((SR, ww), mark[0, s], jnp.int32).astype(F32)
    w_own = wt[own_r, 0:ww]
    grow = gx * hh + row_iota((hh, ww))
    gcol = gy * ww + lane_iota((hh, ww))
    loads[1].wait()
    state[4, own_r, 0:ww] = jnp.where(grow >= 1, level[0].astype(F32) * 0.125 * w_own, 1.0)
    state[5, own_r, 0:ww] = jnp.where(gcol >= 1, level[1].astype(F32) * 0.125 * w_own, 1.0)
    wsend[0] = wt[HALO : HALO + 8, 0:128]
    wsend[1] = wt[HALO + hh - 8 : HALO + hh, 0:128]
    loads[2].wait()
    loads[3].wait()
    acc_l = jnp.zeros((hh, 128), F32)
    acc_r = jnp.zeros((hh, 128), F32)
    for f in range(7):
        field = state.at[f] if f < 6 else wt
        first, last = field[own_r, 0:128], field[own_r, ww - 128 : ww]
        here = (lane >= 8 * f) & (lane < 8 * f + 8)
        first = pltpu.roll(first, 8 * f, 1) if f else first
        acc_l = jnp.where(here, first, acc_l)
        acc_r = jnp.where(here, pltpu.roll(last, 8 * f + 8, 1), acc_r)
        if f < 6:
            rowsend[0, f] = field[HALO : HALO + 8, 0:ww]
            rowsend[1, f] = field[HALO + hh - 8 : HALO + hh, 0:ww]
    pk_l[...] = acc_l
    pk_r[...] = acc_r

    lane_c = lane_iota((rpd, 128))

    def chunk(value, k):
        after = value[:, (cw * (k + 1)) % (cw * n_gy) :][:, 0:128]
        before = value[:, (cw * k - 128) % (cw * n_gy) :][:, 0:128]
        return value[:, cw * k : cw * k + cw], jnp.where(lane_c < 64, after, before)

    for i in (0, 4, 5, 6):
        loads[i].wait()
    t_own = warm[...]
    base = store[...] + film[...]
    force_own = store[...] * t_own + film[...] * bath[...]
    for k in range(n_gy):
        main, edge = chunk(t_own, k)
        tsend[k, :, 0:cw] = main
        tsend[k, :, cw : cw + 128] = edge
        for q, val in enumerate((base, force_own)):
            main, edge = chunk(val, k)
            asend[k, q, :, 0:cw] = main
            asend[k, q, :, cw : cw + 128] = edge

    pl.semaphore_wait(barrier, ndev - 1)

    def remote(src, dst, ssem, rsem, where):
        return pltpu.make_async_remote_copy(
            src_ref=src, dst_ref=dst, send_sem=ssem, recv_sem=rsem, device_id=where,
            device_id_type=MESH,
        )

    def neighbours(send_l, send_r, row_u, row_d, recv_l, recv_r, got_u, got_d, rows, ssem, rsem):
        top, end = slice(0, 8), slice(rows - 8, rows)
        lo, mid, hi = slice(0, 8), slice(8, rows + 8), slice(rows + 8, rows + 16)
        return [
            remote(row_u, got_d, ssem.at[0], rsem.at[0], (up, gy)),
            remote(row_d, got_u, ssem.at[1], rsem.at[1], (down, gy)),
            remote(send_l, recv_r.at[mid], ssem.at[2], rsem.at[2], (gx, left)),
            remote(send_r, recv_l.at[mid], ssem.at[3], rsem.at[3], (gx, right)),
            remote(send_l.at[top], recv_r.at[hi], ssem.at[4], rsem.at[4], (up, left)),
            remote(send_r.at[top], recv_l.at[hi], ssem.at[5], rsem.at[5], (up, right)),
            remote(send_l.at[end], recv_r.at[lo], ssem.at[6], rsem.at[6], (down, left)),
            remote(send_r.at[end], recv_l.at[lo], ssem.at[7], rsem.at[7], (down, right)),
        ]

    first = neighbours(
        pk_l,
        pk_r,
        rowsend.at[0],
        rowsend.at[1],
        rk_l,
        rk_r,
        rowrecv.at[0],
        rowrecv.at[1],
        hh,
        nb_send,
        nb_recv,
    ) + [
        remote(wsend.at[0], wrecv.at[1], nb_send.at[8], nb_recv.at[8], (up, gy)),
        remote(wsend.at[1], wrecv.at[0], nb_send.at[9], nb_recv.at[9], (down, gy)),
    ]

    def spread_out(send, recv, sem):
        def along(k, c):
            t = lax.rem(gy + k, n_gy)
            remote(send.at[t], recv.at[gy + hb], sem.at[1], sem.at[0], (gx, t)).start()
            return c

        lax.fori_loop(1, n_gy, along, 0)
        pltpu.make_async_copy(send.at[gy], recv.at[gy + hb], sem.at[0]).start()

        @pl.when(gy < hb)
        def _():
            def go(k, c):
                remote(
                    send.at[k], recv.at[gy + hb + n_gy], sem.at[2], sem.at[0], (up, k)
                ).start()
                return c

            lax.fori_loop(0, n_gy, go, 0)

        @pl.when(gy >= n_gy - hb)
        def _():
            def go(k, c):
                remote(
                    send.at[k], recv.at[gy - (n_gy - hb)], sem.at[3], sem.at[0], (down, k)
                ).start()
                return c

            lax.fori_loop(0, n_gy, go, 0)

    def spread_sent(send, recv, sem):
        part = pl.ds(0, n_gy - 1)
        remote(send.at[part], recv.at[part], sem.at[1], sem.at[0], (gx, right)).wait_send()
        whole = pl.ds(0, n_gy)

        @pl.when(gy < hb)
        def _():
            remote(send, recv.at[whole], sem.at[2], sem.at[0], (up, gy)).wait_send()

        @pl.when(gy >= n_gy - hb)
        def _():
            remote(send, recv.at[whole], sem.at[3], sem.at[0], (down, gy)).wait_send()

    spread_out(tsend, trecv, t_sem)
    for copy in first:
        copy.start()

    pltpu.make_async_copy(trecv, trecv, t_sem.at[0]).wait()

    def late(k, c):
        t = lax.rem(gy + k, n_gy)
        remote(asend.at[t], arecv.at[gy], a_sem.at[1], a_sem.at[0], (gx, t)).start()
        return c

    lax.fori_loop(1, n_gy, late, 0)
    pltpu.make_async_copy(asend.at[gy], arecv.at[gy], a_sem.at[0]).start()
    crows = ch + 16
    for k in range(nsl):
        tc[rpd * k : rpd * k + rpd, :] = trecv[k]
    cshape = (crows, cw + 128)
    crow_i, clane_i = row_iota(cshape), lane_iota(cshape)
    t_all = tc[...]
    p = t_all
    p = jnp.where((gx == 0) & (crow_i < 8), t_all[8:9, :], p)
    p = jnp.where((gx == n_gx - 1) & (crow_i >= ch + 8), t_all[ch + 7 : ch + 8, :], p)
    wide = cw + 128
    q = jnp.where((gy == 0) & (clane_i == wide - 1), pltpu.roll(p, wide - 1, 1), p)
    q = jnp.where((gy == n_gy - 1) & (clane_i == cw), pltpu.roll(p, 1, 1), q)
    even = 0.75 * q + 0.25 * pltpu.roll(q, 1, 0)
    odd = 0.75 * q + 0.25 * pltpu.roll(q, crows - 1, 0)
    frows = hh + 2 * HALO
    need = frows // 2
    ntile = wide // 128
    for t in range(ntile):
        cols = slice(128 * t, 128 * t + 128)
        widebuf[t, pl.ds(0, need, stride=2), :] = even[4 : 4 + need, cols]
        widebuf[t, pl.ds(1, need, stride=2), :] = odd[4 : 4 + need, cols]
    r = jnp.concatenate([widebuf[t] for t in range(ntile)], axis=1)
    ecol = 0.75 * r + 0.25 * pltpu.roll(r, 1, 1)
    ocol = 0.75 * r + 0.25 * pltpu.roll(r, wide - 1, 1)
    k_i, n_i = row_iota((256, 256)), lane_iota((256, 256))
    weave = (n_i == jnp.where(k_i < 128, 2 * k_i, 2 * k_i - 255)).astype(F32)
    stack = jnp.concatenate(
        [
            jnp.concatenate([ecol[:, 128 * t : 128 * t + 128], ocol[:, 128 * t : 128 * t + 128]], 1)
            for t in range(ntile)
        ],
        axis=0,
    )
    woven = full_dot(stack, weave)
    lane_f = lane_iota((frows, 128))
    pieces = [woven[frows * t : frows * t + frows] for t in range(ntile)]
    edge = jnp.where(lane_f < 64, pieces[-1][:, 0:128], pieces[-1][:, 128:256])
    fine = jnp.concatenate(pieces[:-1] + [edge], axis=1)
    fwide = ww + 128
    tx[...] = 0.6 * (0.5 * (fine + pltpu.roll(fine, 1, 0)))
    ty[...] = 0.6 * (0.5 * (fine + pltpu.roll(fine, 1, 1)))

    for copy in first[2:8]:
        copy.wait_recv()
    got_l, got_r = rk_l[...], rk_r[...]
    for f in range(7):
        from_r = pltpu.roll(got_r, 128 - 8 * f, 1) if f else got_r
        from_l = pltpu.roll(got_l, 120 - 8 * f, 1)
        side = jnp.where(lane_f < 8, from_r, jnp.where(lane_f >= 120, from_l, 0.0))
        if f == 5:
            off_l = (gy == 0) & (lane_f >= 64)
            off_r = (gy == n_gy - 1) & (lane_f < 64)
            side = jnp.where(off_l | off_r, 1.0, side)
        target = state.at[f] if f < 6 else wt
        target[:, ww:fwide] = side
    sub = row_iota((8, fwide))
    last_strip = frows // 8 - 1

    def edges(s, old):
        rows = slice(8 * s, 8 * s + 8)
        u0, u1 = state[0, rows, :], state[1, rows, :]
        w = wt[rows, :]
        r0, r1 = pltpu.roll(u0, 1, 0), pltpu.roll(u1, 1, 0)
        p0 = jnp.where(sub == 0, old["r0"], r0) if old else r0
        p1 = jnp.where(sub == 0, old["r1"], r1) if old else r1
        open_x = u0 - p0 - tx[rows, :]
        st = jnp.maximum(open_x, 0.0)
        dx = jnp.maximum(state[4, rows, :], (1.0 - jnp.exp(st * st * -4.0)) * w)
        state[4, rows, :] = dx
        sp = 1.0 - dx
        nx = sp * open_x
        ax = sp * (u1 - p1)
        open_y = u1 - pltpu.roll(u1, 1, 1) - ty[rows, :]
        st = jnp.maximum(open_y, 0.0)
        dy = jnp.maximum(state[5, rows, :], (1.0 - jnp.exp(st * st * -4.0)) * w)
        state[5, rows, :] = dy
        sp = 1.0 - dy
        ny = sp * open_y
        ay = sp * (u0 - pltpu.roll(u0, 1, 1))
        return dict(
            r0=r0, r1=r1, nx=nx, ax=ax, u0=u0, u1=u1,
            sx=pltpu.roll(nx, 7, 0), sa=pltpu.roll(ax, 7, 0),
            fy0=pltpu.roll(ay, fwide - 1, 1) - ay,
            fy1=pltpu.roll(ny, fwide - 1, 1) - ny,
        )

    def advance(s, old, new):
        rows = slice(8 * s, 8 * s + 8)
        nn = jnp.where(sub == 7, new["sx"], old["sx"])
        na = jnp.where(sub == 7, new["sa"], old["sa"])
        f0 = (nn - old["nx"]) + old["fy0"]
        f1 = (na - old["ax"]) + old["fy1"]
        v0, v1 = state[2, rows, :], state[3, rows, :]
        v0 = v0 + 0.4 * (f0 - 0.05 * v0)
        v1 = v1 + 0.4 * (f1 - 0.05 * v1)
        state[2, rows, :] = v0
        state[3, rows, :] = v1
        state[0, rows, :] = old["u0"] + 0.4 * v0
        state[1, rows, :] = old["u1"] + 0.4 * v1

    redo = (slice(8, 16), slice(8 * last_strip - 8, 8 * last_strip))
    for i, rows in enumerate(redo):
        keep[i] = state[:, rows, :]

    def interior(t, c):
        old = None
        for s in range(1, last_strip):
            new = edges(s, old)
            if s == 2:
                hist[t, 0] = new["sx"]
                hist[t, 1] = new["sa"]
            if s == last_strip - 2:
                hist[t, 2] = new["r0"]
                hist[t, 3] = new["r1"]
            if old:
                advance(s - 1, old, new)
            old = new
        advance(last_strip - 1, old, old)
        return c

    lax.fori_loop(0, SUBSTEPS, interior, 0)

    pltpu.make_async_copy(arecv, arecv, a_sem.at[0]).wait()
    for k in range(n_gy):
        for q in range(2):
            acf[q, 8 + rpd * k : 8 + rpd * k + rpd, :] = arecv[k, q]
    coarse_rows = [
        remote(
            acf.at[:, 8:16], acf.at[:, ch + 8 : ch + 16], a_sem.at[2], a_sem.at[4], (up, gy)
        ),
        remote(acf.at[:, ch : ch + 8], acf.at[:, 0:8], a_sem.at[3], a_sem.at[5], (down, gy)),
    ]
    for copy in coarse_rows:
        copy.start()

    for copy in first[0:2] + first[8:10]:
        copy.wait_recv()
    for i, rows in enumerate(redo):
        state[:, rows, :] = keep[i]
    for side_row, at in ((0, 0), (1, hh + HALO)):
        state[:, at : at + 8, 0:ww] = rowrecv[side_row]
        for t in range(ww // 128):
            wt[at : at + 8, 128 * t : 128 * t + 128] = wrecv[side_row]

    @pl.when(gx == 0)
    def _():
        state[4, 0:8, :] = jnp.ones((8, fwide), F32)

    @pl.when(gx == n_gx - 1)
    def _():
        state[4, hh + HALO : hh + HALO + 8, :] = jnp.ones((8, fwide), F32)

    def border(t, c):
        e0 = edges(0, None)
        e1 = edges(1, e0)
        advance(0, e0, e1)
        advance(1, e1, dict(sx=hist[t, 0], sa=hist[t, 1]))
        e8 = edges(last_strip - 1, dict(r0=hist[t, 2], r1=hist[t, 3]))
        e9 = edges(last_strip, e8)
        advance(last_strip - 1, e8, e9)
        advance(last_strip, e9, e9)
        return c

    lax.fori_loop(0, SUBSTEPS, border, 0)

    dam_x = jnp.where(grow >= 1, state[4, own_r, 0:ww], 0.0)
    dam_y = jnp.where(gcol >= 1, state[5, own_r, 0:ww], 0.0)
    both = dam_x + dam_y
    for t in range(ww // 128):
        gap[t] = both[:, 128 * t : 128 * t + 128]
    rows2 = jnp.concatenate(
        [
            gap[t, pl.ds(0, ch, stride=2), :] + gap[t, pl.ds(1, ch, stride=2), :]
            for t in range(ww // 128)
        ],
        axis=1,
    )
    k_i, n_i = row_iota((256, 128)), lane_iota((256, 128))
    pos = (k_i % SEG).astype(F32)
    col = (2 * (n_i % 64)).astype(F32)
    tab = jnp.exp(jnp.abs(pos - col) * (-4.0 / SEG)) + jnp.exp(jnp.abs(pos - col - 1.0) * (-4.0 / SEG))
    tab = jnp.where(k_i // SEG == n_i // 64, tab * (1.0 / SEG), 0.0)
    npair = ww // 256
    glow = full_dot(
        jnp.concatenate([rows2[:, 256 * t : 256 * t + 256] for t in range(npair)], axis=0), tab
    )
    resist = jnp.concatenate([glow[ch * t : ch * t + ch] for t in range(npair)], axis=1)
    cond_own = (1.0 + 0.5 * tc[8 : 8 + ch, 0:cw]) / (1.0 + resist)
    cbuf[...] = cond_own
    second = neighbours(
        cbuf.at[:, 0:128], cbuf.at[:, cw - 128 : cw], cbuf.at[0:8], cbuf.at[ch - 8 : ch],
        ccl, ccr, crow.at[0], crow.at[1], ch, c_send, c_recv,
    )
    for copy in second:
        copy.start()

    dambuf[0] = dam_x.astype(jnp.bfloat16)
    dambuf[1] = dam_y.astype(jnp.bfloat16)
    puts = [
        pltpu.make_async_copy(src, dst, out_sem.at[i])
        for i, (src, dst) in enumerate(
            (
                (state.at[0:2, own_r, 0:ww], o_shift),
                (state.at[2:4, own_r, 0:ww], o_speed),
                (dambuf, o_dam),
                (warmbuf, o_warm),
            )
        )
    ]
    for copy in puts[0:3]:
        copy.start()

    for copy in coarse_rows:
        copy.wait_recv()

    for copy in second:
        copy.wait_recv()
    lane_k = lane_iota((crows, 128))
    cond = jnp.concatenate(
        [
            jnp.concatenate([crow[0], cbuf[...], crow[1]], axis=0),
            jnp.where(lane_k < 64, ccr[...], ccl[...]),
        ],
        axis=1,
    )
    crow_g = gx * ch - 8 + crow_i
    ccol_g = gy * cw + jnp.where(clane_i < cw + 64, clane_i, clane_i - wide)

    def four(x):
        return (
            pltpu.roll(x, 1, 0),
            pltpu.roll(x, crows - 1, 0),
            pltpu.roll(x, 1, 1),
            pltpu.roll(x, wide - 1, 1),
        )

    masks = (
        crow_g >= 1,
        crow_g <= ch * n_gx - 2,
        ccol_g >= 1,
        ccol_g <= cw * n_gy - 2,
    )
    faces = [
        jnp.where(m, 0.5 * (cond + nb), 0.0) for m, nb in zip(masks, four(cond))
    ]
    offsum = faces[0] + faces[1] + faces[2] + faces[3]
    diagonal = acf[0] + offsum
    ratio = offsum / diagonal
    peak = jnp.max(ratio[8 : 8 + ch, 0:cw])
    msend[...] = jnp.full((8, 128), peak, F32)

    def tell(k, c):
        t = lax.rem(me + k, ndev)
        remote(
            msend, mrecv.at[k - 1], m_sem.at[1], m_sem.at[0], (t // n_gy, t % n_gy)
        ).start()
        return c

    lax.fori_loop(1, ndev, tell, 0)

    t_all = tc[...]
    near = sum(f * nb for f, nb in zip(faces, four(t_all)))
    z = (acf[1] - (diagonal * t_all - near)) / diagonal
    faces = [f / diagonal for f in faces]
    for j in range(4):
        if j:
            z = z - sum(f * nb for f, nb in zip(faces, four(z)))
        for k in range(n_gy):
            zsend[k, j] = z[8 + rpd * k : 8 + rpd * k + rpd, 0:cw]

    def home(k, c):
        t = lax.rem(gy + k, n_gy)
        remote(zsend.at[t], zrecv.at[gy], z_sem.at[1], z_sem.at[0], (gx, t)).start()
        return c

    lax.fori_loop(1, n_gy, home, 0)
    pltpu.make_async_copy(zsend.at[gy], zrecv.at[gy], z_sem.at[0]).start()

    pltpu.make_async_copy(mrecv, mrecv, m_sem.at[0]).wait()
    peak = jnp.maximum(jnp.max(mrecv[...], axis=0), msend[...])[0:1, :]
    low, high = 1.0 - peak, 1.0 + peak
    center = 0.5 * (high + low)
    spread = 0.5 * (high - low)
    sigma = center / spread
    rho = 1.0 / sigma
    zero = jnp.zeros_like(center)
    e = [zero + 1.0, zero, zero, zero]
    d = [1.0 / center, zero, zero, zero]
    total = list(d)
    for _ in range(3):
        e = [e[0]] + [e[i] - d[i - 1] for i in range(1, 4)]
        rho_next = 1.0 / (2.0 * sigma - rho)
        d = [rho_next * rho * d[i] + (2.0 * rho_next / spread) * e[i] for i in range(4)]
        total = [a + b for a, b in zip(total, d)]
        rho = rho_next
    total = [jnp.concatenate([c] * (cw // 128), axis=1) for c in total]

    pltpu.make_async_copy(zrecv, zrecv, z_sem.at[0]).wait()
    for k in range(n_gy):
        x = warm[:, cw * k : cw * k + cw]
        for j in range(4):
            x = x + total[j] * zrecv[k, j]
        warmbuf[:, cw * k : cw * k + cw] = x
    puts[3].start()

    for copy in first + second:
        copy.wait_send()
    spread_sent(tsend, trecv, t_sem)
    remote(
        asend.at[pl.ds(0, n_gy - 1)], arecv.at[pl.ds(0, n_gy - 1)], a_sem.at[1], a_sem.at[0],
        (gx, right),
    ).wait_send()
    for copy in coarse_rows:
        copy.wait_send()
    part = pl.ds(0, n_gy - 1)
    remote(zsend.at[part], zrecv.at[part], z_sem.at[1], z_sem.at[0], (gx, right)).wait_send()
    remote(mrecv, mrecv, m_sem.at[1], m_sem.at[0], (gx, right)).wait_send()
    for copy in puts:
        copy.wait()


def put_out(*refs):
    src, dst, via, (isem, osem) = refs[0:4], refs[4:8], refs[8:12], refs[12:14]
    into = [pltpu.make_async_copy(src[i], via[i], isem.at[i]) for i in range(4)]
    out = [pltpu.make_async_copy(via[i], dst[i], osem.at[i]) for i in range(4)]
    for copy in into:
        copy.start()
    for i in range(4):
        into[i].wait()
        out[i].start()
    for copy in out:
        copy.wait()


def per_device(n_gx, n_gy, shift, speed, level, mark, warm, store, film, bath):
    _, hh, ww = shift.shape
    rpd, _ = warm.shape
    cw, ch = ww // 2, hh // 2
    wide, fwide = cw + 128, ww + 128
    crows, frows = ch + 16, hh + 2 * HALO
    nsl = n_gy + 2 * (HALO // rpd)
    vm = lambda *s: pltpu.VMEM(s, F32)
    dma = lambda n: pltpu.SemaphoreType.DMA((n,))
    hbm = pl.BlockSpec(memory_space=pltpu.HBM)
    outs = pl.pallas_call(
        functools.partial(kernel, n_gx, n_gy),
        out_shape=(
            jax.ShapeDtypeStruct(shift.shape, F32),
            jax.ShapeDtypeStruct(speed.shape, F32),
            jax.ShapeDtypeStruct(level.shape, jnp.bfloat16),
            jax.ShapeDtypeStruct(warm.shape, F32),
        ),
        in_specs=[hbm] * 3 + [pl.BlockSpec(memory_space=pltpu.SMEM)] + [hbm] * 4,
        out_specs=(hbm,) * 4,
        scratch_shapes=[
            vm(n_gy, rpd, wide),
            vm(nsl, rpd, wide),
            vm(n_gy, 2, rpd, wide),
            vm(n_gy, 2, rpd, wide),
            vm(hh, 128),
            vm(hh, 128),
            vm(frows, 128),
            vm(frows, 128),
            vm(2, 8, 128),
            vm(2, 8, 128),
            vm(2, 6, 8, ww),
            vm(2, 6, 8, ww),
            vm(2, 6, 8, fwide),
            vm(SUBSTEPS, 4, 8, fwide),
            pltpu.VMEM(level.shape, level.dtype),
            vm(*warm.shape),
            vm(*warm.shape),
            vm(*warm.shape),
            vm(*warm.shape),
            vm(6, frows, fwide),
            vm(frows, fwide),
            vm(frows, fwide),
            vm(frows, fwide),
            vm(crows, wide),
            vm(2, crows, wide),
            vm(wide // 128, frows, 128),
            vm(ww // 128, hh, 128),
            vm(ch, cw),
            vm(2, 8, cw),
            vm(crows, 128),
            vm(crows, 128),
            vm(n_gy, 4, rpd, cw),
            vm(n_gy, 4, rpd, cw),
            vm(8, 128),
            vm(n_gx * n_gy - 1, 8, 128),
            dma(10),
            dma(10),
            dma(4),
            dma(6),
            dma(8),
            dma(8),
            dma(2),
            dma(2),
            dma(7),
            pltpu.VMEM(level.shape, jnp.bfloat16),
            vm(*warm.shape),
            dma(4),
        ],
        compiler_params=pltpu.CompilerParams(
            collective_id=0, has_side_effects=True
        ),
    )(shift, speed, level, mark.reshape(1, hh // SR), warm, store, film, bath)
    return pl.pallas_call(
        put_out,
        out_shape=tuple(jax.ShapeDtypeStruct(o.shape, o.dtype) for o in outs),
        in_specs=[hbm] * 4,
        out_specs=(hbm,) * 4,
        scratch_shapes=[pltpu.VMEM(o.shape, o.dtype) for o in outs] + [dma(4), dma(4)],
    )(*outs)


def solution(mesh):
    rows = P(("gx", "gy"), None)
    plate = P(None, "gx", "gy")
    return jax.shard_map(
        functools.partial(per_device, mesh.shape["gx"], mesh.shape["gy"]),
        mesh=mesh,
        in_specs=(plate, plate, plate, P("gx", "gy"), rows, rows, rows, rows),
        out_specs=(plate, plate, plate, rows),
        check_vma=False,
    )
```

```python
import functools

import jax
import jax.numpy as jnp
from jax import lax
from jax.experimental import pallas as pl
from jax.experimental.pallas import tpu as pltpu
from jax.sharding import PartitionSpec as P

SR = 8
SEG = 128
SUBSTEPS = 8
HALO = 8
MESH = pl.DeviceIdType.MESH
F32 = jnp.float32


def lane_iota(shape):
    return lax.broadcasted_iota(jnp.int32, shape, 1)


def row_iota(shape):
    return lax.broadcasted_iota(jnp.int32, shape, 0)


def full_dot(a, b):
    return jnp.dot(a, b, precision=lax.Precision.HIGHEST, preferred_element_type=F32)


def kernel(
    n_gx,
    n_gy,
    shift,
    speed,
    level_h,
    mark,
    warm_h,
    store_h,
    film_h,
    bath_h,
    o_shift,
    o_speed,
    o_dam,
    o_warm,
    tsend,
    trecv,
    asend,
    arecv,
    pk_l,
    pk_r,
    rk_l,
    rk_r,
    wsend,
    wrecv,
    rowsend,
    rowrecv,
    keep,
    hist,
    level,
    warm,
    store,
    film,
    bath,
    state,
    wt,
    tx,
    ty,
    tc,
    acf,
    widebuf,
    gap,
    cbuf,
    crow,
    ccl,
    ccr,
    zsend,
    zrecv,
    msend,
    mrecv,
    nb_send,
    nb_recv,
    t_sem,
    a_sem,
    c_send,
    c_recv,
    z_sem,
    m_sem,
    in_sem,
    dambuf,
    warmbuf,
    out_sem,
):
    ndev = n_gx * n_gy
    gx = lax.axis_index("gx")
    gy = lax.axis_index("gy")
    me = gx * n_gy + gy
    _, hh, ww = shift.shape
    rpd, _ = warm_h.shape
    cw = ww // 2
    ch = hh // 2
    hb = HALO // rpd
    nsl = n_gy + 2 * hb
    up = lax.rem(gx + n_gx - 1, n_gx)
    down = lax.rem(gx + 1, n_gx)
    left = lax.rem(gy + n_gy - 1, n_gy)
    right = lax.rem(gy + 1, n_gy)

    own_r = slice(HALO, HALO + hh)
    loads = [
        pltpu.make_async_copy(src, dst, in_sem.at[i])
        for i, (src, dst) in enumerate(
            (
                (warm_h, warm),
                (level_h, level),
                (shift, state.at[0:2, own_r, 0:ww]),
                (speed, state.at[2:4, own_r, 0:ww]),
                (store_h, store),
                (film_h, film),
                (bath_h, bath),
            )
        )
    ]
    for copy in loads:
        copy.start()
    barrier = pltpu.get_barrier_semaphore()

    def greet(k, c):
        t = lax.rem(me + k, ndev)
        pl.semaphore_signal(barrier, inc=1, device_id=(t // n_gy, t % n_gy), device_id_type=MESH)
        return c

    lax.fori_loop(1, ndev, greet, 0)

    lane = lane_iota((hh, 128))
    for s in range(hh // SR):
        wt[HALO + SR * s : HALO + SR * s + SR, 0:ww] = jnp.full((SR, ww), mark[0, s], jnp.int32).astype(F32)
    w_own = wt[own_r, 0:ww]
    grow = gx * hh + row_iota((hh, ww))
    gcol = gy * ww + lane_iota((hh, ww))
    loads[1].wait()
    state[4, own_r, 0:ww] = jnp.where(grow >= 1, level[0].astype(F32) * 0.125 * w_own, 1.0)
    state[5, own_r, 0:ww] = jnp.where(gcol >= 1, level[1].astype(F32) * 0.125 * w_own, 1.0)
    wsend[0] = wt[HALO : HALO + 8, 0:128]
    wsend[1] = wt[HALO + hh - 8 : HALO + hh, 0:128]
    loads[2].wait()
    loads[3].wait()
    acc_l = jnp.zeros((hh, 128), F32)
    acc_r = jnp.zeros((hh, 128), F32)
    for f in range(7):
        field = state.at[f] if f < 6 else wt
        first, last = field[own_r, 0:128], field[own_r, ww - 128 : ww]
        here = (lane >= 8 * f) & (lane < 8 * f + 8)
        first = pltpu.roll(first, 8 * f, 1) if f else first
        acc_l = jnp.where(here, first, acc_l)
        acc_r = jnp.where(here, pltpu.roll(last, 8 * f + 8, 1), acc_r)
        if f < 6:
            rowsend[0, f] = field[HALO : HALO + 8, 0:ww]
            rowsend[1, f] = field[HALO + hh - 8 : HALO + hh, 0:ww]
    pk_l[...] = acc_l
    pk_r[...] = acc_r

    lane_c = lane_iota((rpd, 128))

    def chunk(value, k):
        after = value[:, (cw * (k + 1)) % (cw * n_gy) :][:, 0:128]
        before = value[:, (cw * k - 128) % (cw * n_gy) :][:, 0:128]
        return value[:, cw * k : cw * k + cw], jnp.where(lane_c < 64, after, before)

    for i in (0, 4, 5, 6):
        loads[i].wait()
    t_own = warm[...]
    base = store[...] + film[...]
    force_own = store[...] * t_own + film[...] * bath[...]
    for k in range(n_gy):
        main, edge = chunk(t_own, k)
        tsend[k, :, 0:cw] = main
        tsend[k, :, cw : cw + 128] = edge
        for q, val in enumerate((base, force_own)):
            main, edge = chunk(val, k)
            asend[k, q, :, 0:cw] = main
            asend[k, q, :, cw : cw + 128] = edge

    pl.semaphore_wait(barrier, ndev - 1)

    def remote(src, dst, ssem, rsem, where):
        return pltpu.make_async_remote_copy(
            src_ref=src, dst_ref=dst, send_sem=ssem, recv_sem=rsem, device_id=where,
            device_id_type=MESH,
        )

    def neighbours(send_l, send_r, row_u, row_d, recv_l, recv_r, got_u, got_d, rows, ssem, rsem):
        top, end = slice(0, 8), slice(rows - 8, rows)
        lo, mid, hi = slice(0, 8), slice(8, rows + 8), slice(rows + 8, rows + 16)
        return [
            remote(row_u, got_d, ssem.at[0], rsem.at[0], (up, gy)),
            remote(row_d, got_u, ssem.at[1], rsem.at[1], (down, gy)),
            remote(send_l, recv_r.at[mid], ssem.at[2], rsem.at[2], (gx, left)),
            remote(send_r, recv_l.at[mid], ssem.at[3], rsem.at[3], (gx, right)),
            remote(send_l.at[top], recv_r.at[hi], ssem.at[4], rsem.at[4], (up, left)),
            remote(send_r.at[top], recv_l.at[hi], ssem.at[5], rsem.at[5], (up, right)),
            remote(send_l.at[end], recv_r.at[lo], ssem.at[6], rsem.at[6], (down, left)),
            remote(send_r.at[end], recv_l.at[lo], ssem.at[7], rsem.at[7], (down, right)),
        ]

    first = neighbours(
        pk_l,
        pk_r,
        rowsend.at[0],
        rowsend.at[1],
        rk_l,
        rk_r,
        rowrecv.at[0],
        rowrecv.at[1],
        hh,
        nb_send,
        nb_recv,
    ) + [
        remote(wsend.at[0], wrecv.at[1], nb_send.at[8], nb_recv.at[8], (up, gy)),
        remote(wsend.at[1], wrecv.at[0], nb_send.at[9], nb_recv.at[9], (down, gy)),
    ]

    def spread_out(send, recv, sem):
        def along(k, c):
            t = lax.rem(gy + k, n_gy)
            remote(send.at[t], recv.at[gy + hb], sem.at[1], sem.at[0], (gx, t)).start()
            return c

        lax.fori_loop(1, n_gy, along, 0)
        pltpu.make_async_copy(send.at[gy], recv.at[gy + hb], sem.at[0]).start()

        @pl.when(gy < hb)
        def _():
            def go(k, c):
                remote(
                    send.at[k], recv.at[gy + hb + n_gy], sem.at[2], sem.at[0], (up, k)
                ).start()
                return c

            lax.fori_loop(0, n_gy, go, 0)

        @pl.when(gy >= n_gy - hb)
        def _():
            def go(k, c):
                remote(
                    send.at[k], recv.at[gy - (n_gy - hb)], sem.at[3], sem.at[0], (down, k)
                ).start()
                return c

            lax.fori_loop(0, n_gy, go, 0)

    def spread_sent(send, recv, sem):
        part = pl.ds(0, n_gy - 1)
        remote(send.at[part], recv.at[part], sem.at[1], sem.at[0], (gx, right)).wait_send()
        whole = pl.ds(0, n_gy)

        @pl.when(gy < hb)
        def _():
            remote(send, recv.at[whole], sem.at[2], sem.at[0], (up, gy)).wait_send()

        @pl.when(gy >= n_gy - hb)
        def _():
            remote(send, recv.at[whole], sem.at[3], sem.at[0], (down, gy)).wait_send()

    spread_out(tsend, trecv, t_sem)
    for copy in first:
        copy.start()

    pltpu.make_async_copy(trecv, trecv, t_sem.at[0]).wait()

    def late(k, c):
        t = lax.rem(gy + k, n_gy)
        remote(asend.at[t], arecv.at[gy], a_sem.at[1], a_sem.at[0], (gx, t)).start()
        return c

    lax.fori_loop(1, n_gy, late, 0)
    pltpu.make_async_copy(asend.at[gy], arecv.at[gy], a_sem.at[0]).start()
    crows = ch + 16
    for k in range(nsl):
        tc[rpd * k : rpd * k + rpd, :] = trecv[k]
    cshape = (crows, cw + 128)
    crow_i, clane_i = row_iota(cshape), lane_iota(cshape)
    t_all = tc[...]
    p = t_all
    p = jnp.where((gx == 0) & (crow_i < 8), t_all[8:9, :], p)
    p = jnp.where((gx == n_gx - 1) & (crow_i >= ch + 8), t_all[ch + 7 : ch + 8, :], p)
    wide = cw + 128
    q = jnp.where((gy == 0) & (clane_i == wide - 1), pltpu.roll(p, wide - 1, 1), p)
    q = jnp.where((gy == n_gy - 1) & (clane_i == cw), pltpu.roll(p, 1, 1), q)
    even = 0.75 * q + 0.25 * pltpu.roll(q, 1, 0)
    odd = 0.75 * q + 0.25 * pltpu.roll(q, crows - 1, 0)
    frows = hh + 2 * HALO
    need = frows // 2
    ntile = wide // 128
    for t in range(ntile):
        cols = slice(128 * t, 128 * t + 128)
        widebuf[t, pl.ds(0, need, stride=2), :] = even[4 : 4 + need, cols]
        widebuf[t, pl.ds(1, need, stride=2), :] = odd[4 : 4 + need, cols]
    r = jnp.concatenate([widebuf[t] for t in range(ntile)], axis=1)
    ecol = 0.75 * r + 0.25 * pltpu.roll(r, 1, 1)
    ocol = 0.75 * r + 0.25 * pltpu.roll(r, wide - 1, 1)
    k_i, n_i = row_iota((256, 256)), lane_iota((256, 256))
    weave = (n_i == jnp.where(k_i < 128, 2 * k_i, 2 * k_i - 255)).astype(F32)
    stack = jnp.concatenate(
        [
            jnp.concatenate([ecol[:, 128 * t : 128 * t + 128], ocol[:, 128 * t : 128 * t + 128]], 1)
            for t in range(ntile)
        ],
        axis=0,
    )
    woven = full_dot(stack, weave)
    lane_f = lane_iota((frows, 128))
    pieces = [woven[frows * t : frows * t + frows] for t in range(ntile)]
    edge = jnp.where(lane_f < 64, pieces[-1][:, 0:128], pieces[-1][:, 128:256])
    fine = jnp.concatenate(pieces[:-1] + [edge], axis=1)
    fwide = ww + 128
    tx[...] = 0.6 * (0.5 * (fine + pltpu.roll(fine, 1, 0)))
    ty[...] = 0.6 * (0.5 * (fine + pltpu.roll(fine, 1, 1)))

    for copy in first[2:8]:
        copy.wait_recv()
    got_l, got_r = rk_l[...], rk_r[...]
    for f in range(7):
        from_r = pltpu.roll(got_r, 128 - 8 * f, 1) if f else got_r
        from_l = pltpu.roll(got_l, 120 - 8 * f, 1)
        side = jnp.where(lane_f < 8, from_r, jnp.where(lane_f >= 120, from_l, 0.0))
        if f == 5:
            off_l = (gy == 0) & (lane_f >= 64)
            off_r = (gy == n_gy - 1) & (lane_f < 64)
            side = jnp.where(off_l | off_r, 1.0, side)
        target = state.at[f] if f < 6 else wt
        target[:, ww:fwide] = side
    sub = row_iota((8, fwide))
    last_strip = frows // 8 - 1

    def edges(s, old):
        rows = slice(8 * s, 8 * s + 8)
        u0, u1 = state[0, rows, :], state[1, rows, :]
        w = wt[rows, :]
        r0, r1 = pltpu.roll(u0, 1, 0), pltpu.roll(u1, 1, 0)
        p0 = jnp.where(sub == 0, old["r0"], r0) if old else r0
        p1 = jnp.where(sub == 0, old["r1"], r1) if old else r1
        open_x = u0 - p0 - tx[rows, :]
        st = jnp.maximum(open_x, 0.0)
        dx = jnp.maximum(state[4, rows, :], (1.0 - jnp.exp(st * st * -4.0)) * w)
        state[4, rows, :] = dx
        sp = 1.0 - dx
        nx = sp * open_x
        ax = sp * (u1 - p1)
        open_y = u1 - pltpu.roll(u1, 1, 1) - ty[rows, :]
        st = jnp.maximum(open_y, 0.0)
        dy = jnp.maximum(state[5, rows, :], (1.0 - jnp.exp(st * st * -4.0)) * w)
        state[5, rows, :] = dy
        sp = 1.0 - dy
        ny = sp * open_y
        ay = sp * (u0 - pltpu.roll(u0, 1, 1))
        return dict(
            r0=r0, r1=r1, nx=nx, ax=ax, u0=u0, u1=u1,
            sx=pltpu.roll(nx, 7, 0), sa=pltpu.roll(ax, 7, 0),
            fy0=pltpu.roll(ay, fwide - 1, 1) - ay,
            fy1=pltpu.roll(ny, fwide - 1, 1) - ny,
        )

    def advance(s, old, new):
        rows = slice(8 * s, 8 * s + 8)
        nn = jnp.where(sub == 7, new["sx"], old["sx"])
        na = jnp.where(sub == 7, new["sa"], old["sa"])
        f0 = (nn - old["nx"]) + old["fy0"]
        f1 = (na - old["ax"]) + old["fy1"]
        v0, v1 = state[2, rows, :], state[3, rows, :]
        v0 = v0 + 0.4 * (f0 - 0.05 * v0)
        v1 = v1 + 0.4 * (f1 - 0.05 * v1)
        state[2, rows, :] = v0
        state[3, rows, :] = v1
        state[0, rows, :] = old["u0"] + 0.4 * v0
        state[1, rows, :] = old["u1"] + 0.4 * v1

    redo = (slice(8, 16), slice(8 * last_strip - 8, 8 * last_strip))
    for i, rows in enumerate(redo):
        keep[i] = state[:, rows, :]

    def interior(t, c):
        old = None
        for s in range(1, last_strip):
            new = edges(s, old)
            if s == 2:
                hist[t, 0] = new["sx"]
                hist[t, 1] = new["sa"]
            if s == last_strip - 2:
                hist[t, 2] = new["r0"]
                hist[t, 3] = new["r1"]
            if old:
                advance(s - 1, old, new)
            old = new
        advance(last_strip - 1, old, old)
        return c

    lax.fori_loop(0, SUBSTEPS, interior, 0)

    pltpu.make_async_copy(arecv, arecv, a_sem.at[0]).wait()
    for k in range(n_gy):
        for q in range(2):
            acf[q, 8 + rpd * k : 8 + rpd * k + rpd, :] = arecv[k, q]
    coarse_rows = [
        remote(
            acf.at[:, 8:16], acf.at[:, ch + 8 : ch + 16], a_sem.at[2], a_sem.at[4], (up, gy)
        ),
        remote(acf.at[:, ch : ch + 8], acf.at[:, 0:8], a_sem.at[3], a_sem.at[5], (down, gy)),
    ]
    for copy in coarse_rows:
        copy.start()

    for copy in first[0:2] + first[8:10]:
        copy.wait_recv()
    for i, rows in enumerate(redo):
        state[:, rows, :] = keep[i]
    for side_row, at in ((0, 0), (1, hh + HALO)):
        state[:, at : at + 8, 0:ww] = rowrecv[side_row]
        for t in range(ww // 128):
            wt[at : at + 8, 128 * t : 128 * t + 128] = wrecv[side_row]

    @pl.when(gx == 0)
    def _():
        state[4, 0:8, :] = jnp.ones((8, fwide), F32)

    @pl.when(gx == n_gx - 1)
    def _():
        state[4, hh + HALO : hh + HALO + 8, :] = jnp.ones((8, fwide), F32)

    def border(t, c):
        e0 = edges(0, None)
        e1 = edges(1, e0)
        advance(0, e0, e1)
        advance(1, e1, dict(sx=hist[t, 0], sa=hist[t, 1]))
        e8 = edges(last_strip - 1, dict(r0=hist[t, 2], r1=hist[t, 3]))
        e9 = edges(last_strip, e8)
        advance(last_strip - 1, e8, e9)
        advance(last_strip, e9, e9)
        return c

    lax.fori_loop(0, SUBSTEPS, border, 0)

    dam_x = jnp.where(grow >= 1, state[4, own_r, 0:ww], 0.0)
    dam_y = jnp.where(gcol >= 1, state[5, own_r, 0:ww], 0.0)
    both = dam_x + dam_y
    for t in range(ww // 128):
        gap[t] = both[:, 128 * t : 128 * t + 128]
    rows2 = jnp.concatenate(
        [
            gap[t, pl.ds(0, ch, stride=2), :] + gap[t, pl.ds(1, ch, stride=2), :]
            for t in range(ww // 128)
        ],
        axis=1,
    )
    k_i, n_i = row_iota((256, 128)), lane_iota((256, 128))
    pos = (k_i % SEG).astype(F32)
    col = (2 * (n_i % 64)).astype(F32)
    tab = jnp.exp(jnp.abs(pos - col) * (-4.0 / SEG)) + jnp.exp(jnp.abs(pos - col - 1.0) * (-4.0 / SEG))
    tab = jnp.where(k_i // SEG == n_i // 64, tab * (1.0 / SEG), 0.0)
    npair = ww // 256
    glow = full_dot(
        jnp.concatenate([rows2[:, 256 * t : 256 * t + 256] for t in range(npair)], axis=0), tab
    )
    resist = jnp.concatenate([glow[ch * t : ch * t + ch] for t in range(npair)], axis=1)
    cond_own = (1.0 + 0.5 * tc[8 : 8 + ch, 0:cw]) / (1.0 + resist)
    cbuf[...] = cond_own
    second = neighbours(
        cbuf.at[:, 0:128], cbuf.at[:, cw - 128 : cw], cbuf.at[0:8], cbuf.at[ch - 8 : ch],
        ccl, ccr, crow.at[0], crow.at[1], ch, c_send, c_recv,
    )
    for copy in second:
        copy.start()

    dambuf[0] = dam_x.astype(jnp.bfloat16)
    dambuf[1] = dam_y.astype(jnp.bfloat16)
    puts = [
        pltpu.make_async_copy(src, dst, out_sem.at[i])
        for i, (src, dst) in enumerate(
            (
                (state.at[0:2, own_r, 0:ww], o_shift),
                (state.at[2:4, own_r, 0:ww], o_speed),
                (dambuf, o_dam),
                (warmbuf, o_warm),
            )
        )
    ]
    for copy in puts[0:3]:
        copy.start()

    for copy in coarse_rows:
        copy.wait_recv()

    for copy in second:
        copy.wait_recv()
    lane_k = lane_iota((crows, 128))
    cond = jnp.concatenate(
        [
            jnp.concatenate([crow[0], cbuf[...], crow[1]], axis=0),
            jnp.where(lane_k < 64, ccr[...], ccl[...]),
        ],
        axis=1,
    )
    crow_g = gx * ch - 8 + crow_i
    ccol_g = gy * cw + jnp.where(clane_i < cw + 64, clane_i, clane_i - wide)

    def four(x):
        return (
            pltpu.roll(x, 1, 0),
            pltpu.roll(x, crows - 1, 0),
            pltpu.roll(x, 1, 1),
            pltpu.roll(x, wide - 1, 1),
        )

    masks = (
        crow_g >= 1,
        crow_g <= ch * n_gx - 2,
        ccol_g >= 1,
        ccol_g <= cw * n_gy - 2,
    )
    faces = [
        jnp.where(m, 0.5 * (cond + nb), 0.0) for m, nb in zip(masks, four(cond))
    ]
    offsum = faces[0] + faces[1] + faces[2] + faces[3]
    diagonal = acf[0] + offsum
    ratio = offsum / diagonal
    peak = jnp.max(ratio[8 : 8 + ch, 0:cw])
    msend[...] = jnp.full((1, 128), peak, F32)

    def tell(k, c):
        t = lax.rem(me + k, ndev)
        remote(
            msend, mrecv.at[k - 1], m_sem.at[1], m_sem.at[0], (t // n_gy, t % n_gy)
        ).start()
        return c

    lax.fori_loop(1, ndev, tell, 0)

    t_all = tc[...]
    near = sum(f * nb for f, nb in zip(faces, four(t_all)))
    z = (acf[1] - (diagonal * t_all - near)) / diagonal
    faces = [f / diagonal for f in faces]
    for j in range(4):
        if j:
            z = z - sum(f * nb for f, nb in zip(faces, four(z)))
        for k in range(n_gy):
            zsend[k, j] = z[8 + rpd * k : 8 + rpd * k + rpd, 0:cw]

    def home(k, c):
        t = lax.rem(gy + k, n_gy)
        remote(zsend.at[t], zrecv.at[gy], z_sem.at[1], z_sem.at[0], (gx, t)).start()
        return c

    lax.fori_loop(1, n_gy, home, 0)
    pltpu.make_async_copy(zsend.at[gy], zrecv.at[gy], z_sem.at[0]).start()

    pltpu.make_async_copy(mrecv, mrecv, m_sem.at[0]).wait()
    peak = jnp.maximum(jnp.max(mrecv[...], axis=0), msend[...])[0:1, :]
    low, high = 1.0 - peak, 1.0 + peak
    center = 0.5 * (high + low)
    spread = 0.5 * (high - low)
    sigma = center / spread
    rho = 1.0 / sigma
    zero = jnp.zeros_like(center)
    e = [zero + 1.0, zero, zero, zero]
    d = [1.0 / center, zero, zero, zero]
    total = list(d)
    for _ in range(3):
        e = [e[0]] + [e[i] - d[i - 1] for i in range(1, 4)]
        rho_next = 1.0 / (2.0 * sigma - rho)
        d = [rho_next * rho * d[i] + (2.0 * rho_next / spread) * e[i] for i in range(4)]
        total = [a + b for a, b in zip(total, d)]
        rho = rho_next
    total = [jnp.concatenate([c] * (cw // 128), axis=1) for c in total]

    pltpu.make_async_copy(zrecv, zrecv, z_sem.at[0]).wait()
    for k in range(n_gy):
        x = warm[:, cw * k : cw * k + cw]
        for j in range(4):
            x = x + total[j] * zrecv[k, j]
        warmbuf[:, cw * k : cw * k + cw] = x
    puts[3].start()

    for copy in first + second:
        copy.wait_send()
    spread_sent(tsend, trecv, t_sem)
    remote(
        asend.at[pl.ds(0, n_gy - 1)], arecv.at[pl.ds(0, n_gy - 1)], a_sem.at[1], a_sem.at[0],
        (gx, right),
    ).wait_send()
    for copy in coarse_rows:
        copy.wait_send()
    part = pl.ds(0, n_gy - 1)
    remote(zsend.at[part], zrecv.at[part], z_sem.at[1], z_sem.at[0], (gx, right)).wait_send()
    remote(mrecv, mrecv, m_sem.at[1], m_sem.at[0], (gx, right)).wait_send()
    for copy in puts:
        copy.wait()


def put_out(*refs):
    src, dst, via, (isem, osem) = refs[0:4], refs[4:8], refs[8:12], refs[12:14]
    into = [pltpu.make_async_copy(src[i], via[i], isem.at[i]) for i in range(4)]
    out = [pltpu.make_async_copy(via[i], dst[i], osem.at[i]) for i in range(4)]
    for copy in into:
        copy.start()
    for i in range(4):
        into[i].wait()
        out[i].start()
    for copy in out:
        copy.wait()


def per_device(n_gx, n_gy, shift, speed, level, mark, warm, store, film, bath):
    _, hh, ww = shift.shape
    rpd, _ = warm.shape
    cw, ch = ww // 2, hh // 2
    wide, fwide = cw + 128, ww + 128
    crows, frows = ch + 16, hh + 2 * HALO
    nsl = n_gy + 2 * (HALO // rpd)
    vm = lambda *s: pltpu.VMEM(s, F32)
    dma = lambda n: pltpu.SemaphoreType.DMA((n,))
    hbm = pl.BlockSpec(memory_space=pltpu.HBM)
    outs = pl.pallas_call(
        functools.partial(kernel, n_gx, n_gy),
        out_shape=(
            jax.ShapeDtypeStruct(shift.shape, F32),
            jax.ShapeDtypeStruct(speed.shape, F32),
            jax.ShapeDtypeStruct(level.shape, jnp.bfloat16),
            jax.ShapeDtypeStruct(warm.shape, F32),
        ),
        in_specs=[hbm] * 3 + [pl.BlockSpec(memory_space=pltpu.SMEM)] + [hbm] * 4,
        out_specs=(hbm,) * 4,
        scratch_shapes=[
            vm(n_gy, rpd, wide),
            vm(nsl, rpd, wide),
            vm(n_gy, 2, rpd, wide),
            vm(n_gy, 2, rpd, wide),
            vm(hh, 128),
            vm(hh, 128),
            vm(frows, 128),
            vm(frows, 128),
            vm(2, 8, 128),
            vm(2, 8, 128),
            vm(2, 6, 8, ww),
            vm(2, 6, 8, ww),
            vm(2, 6, 8, fwide),
            vm(SUBSTEPS, 4, 8, fwide),
            pltpu.VMEM(level.shape, level.dtype),
            vm(*warm.shape),
            vm(*warm.shape),
            vm(*warm.shape),
            vm(*warm.shape),
            vm(6, frows, fwide),
            vm(frows, fwide),
            vm(frows, fwide),
            vm(frows, fwide),
            vm(crows, wide),
            vm(2, crows, wide),
            vm(wide // 128, frows, 128),
            vm(ww // 128, hh, 128),
            vm(ch, cw),
            vm(2, 8, cw),
            vm(crows, 128),
            vm(crows, 128),
            vm(n_gy, 4, rpd, cw),
            vm(n_gy, 4, rpd, cw),
            vm(1, 128),
            vm(n_gx * n_gy - 1, 1, 128),
            dma(10),
            dma(10),
            dma(4),
            dma(6),
            dma(8),
            dma(8),
            dma(2),
            dma(2),
            dma(7),
            pltpu.VMEM(level.shape, jnp.bfloat16),
            vm(*warm.shape),
            dma(4),
        ],
        compiler_params=pltpu.CompilerParams(
            collective_id=0, has_side_effects=True
        ),
    )(shift, speed, level, mark.reshape(1, hh // SR), warm, store, film, bath)
    return pl.pallas_call(
        put_out,
        out_shape=tuple(jax.ShapeDtypeStruct(o.shape, o.dtype) for o in outs),
        in_specs=[hbm] * 4,
        out_specs=(hbm,) * 4,
        scratch_shapes=[pltpu.VMEM(o.shape, o.dtype) for o in outs] + [dma(4), dma(4)],
    )(*outs)


def solution(mesh):
    rows = P(("gx", "gy"), None)
    plate = P(None, "gx", "gy")
    return jax.shard_map(
        functools.partial(per_device, mesh.shape["gx"], mesh.shape["gy"]),
        mesh=mesh,
        in_specs=(plate, plate, plate, P("gx", "gy"), rows, rows, rows, rows),
        out_specs=(plate, plate, plate, rows),
        check_vma=False,
    )
```
